512 devices in a mesh: grp: 8 (over y_lo, x), view: 64 (over y_hi, z, core).
Axes of the slice: x: 4, y: 8 (y_hi: 4, y_lo: 2; y = y_hi * 2 + y_lo), z: 8, core: 2. Of those that a mesh axis runs over, the one named last changes fastest.
Arguments:
- volume: float32 [1024, 16, 2, 512], P(('grp', 'view')), may hold values from 0 to 2
- footprint: bfloat16 [1024, 2, 512, 896], P(('grp', 'view')), may hold values from -0.1875 to 0.1875
- measured: bfloat16 [4096, 64, 896], P(('grp', 'view')), may hold values from 0 to 3
- angle_index: int32 [4096], P(('grp', 'view')), may hold values from 0 to 1
- cover: int32 [4096, 4], P(('grp', 'view')), may hold values from 0 to 1023, as said below
- offset: int32 [4096, 4], P(('grp', 'view')), may hold values from 0 to 48
- count: int32 [4096], P(('grp', 'view')), may hold values from 1 to 4
Outputs:
- gradient: float32 [1024, 16, 2, 512], P(('grp', 'view'))
The draws below stay inside these ranges and needn't reach their ends.
Inputs may be any that keep to these rules, and one draw needn't show every extreme that they name: Let p = v // 8. cover[v,k] lies between max(p - 4, 0) * 2 and min(p + 5, 512) * 2 - 1, and both ends are named by some slot 0 of p's views.
All inputs are finite; a program needn't handle non-finite values.
Results may differ from the reference program's by a relative error of at most 0.0019.
Values may be sent and summed in bfloat16 or wider, within the bound.
A program may use at most 64 MiB of HBM per device.

```python
import jax
import jax.numpy as jnp
from jax import lax

VX = 512
YW = 2
DC = 896
DR = 64
BZ = 16
KMAX = 4
REACH = 4
A_DEV = 2
BLK_DEV = 2
V_DEV = 8
NBLOCKS = 1024
VIEWS = 4096
ANGLES = 1024


def draw_cover(key, part):
    devices_all = VIEWS // V_DEV
    views_iota = jnp.arange(VIEWS, dtype=jnp.int32)
    owner = views_iota // V_DEV
    lowest = jnp.maximum(owner - REACH, 0) * BLK_DEV
    highest = jnp.minimum(owner + REACH + 1, devices_all) * BLK_DEV
    spread = highest - lowest
    raw = jax.random.randint(key, (VIEWS, KMAX), 0, 1048576, dtype=jnp.int32)
    picked = lowest[:, None] + raw % spread[:, None]
    first_slot = jnp.arange(KMAX, dtype=jnp.int32)[None, :] == 0
    local_view = (views_iota % V_DEV)[:, None]
    picked = jnp.where(first_slot & (local_view == 0), lowest[:, None], picked)
    picked = jnp.where(first_slot & (local_view == 1), highest[:, None] - 1, picked)
    return picked.astype(jnp.int32)


def plant(values, key, least, top_value):
    dims = values.shape
    place = [jax.random.randint(jax.random.fold_in(key, axis), (), 0, dims[axis]) for axis in range(len(dims))]
    values = values.at[tuple(place)].set(least)
    longest = dims.index(max(dims))
    place[longest] = (place[longest] + 1) % dims[longest]
    return values.at[tuple(place)].set(top_value)


def level_of(rng, extent, cuts, least, top_value):
    loudness, own = 1.0, jax.random.fold_in(rng, 6)
    for dim, shards_of in cuts:
        draws = jnp.exp(jax.random.uniform(jax.random.fold_in(own, dim), (shards_of,), jnp.float32, least / len(cuts), top_value / len(cuts)))
        loudness = loudness * jnp.repeat(draws, extent[dim] // shards_of).reshape([-1 if axis == dim else 1 for axis in range(len(extent))])
    return loudness


def normal_values(rng, extent, width, bound, shards=(), held_as=jnp.bfloat16):
    drawn = width * jax.random.normal(rng, extent, jnp.float32)
    if shards:
        drawn = drawn * level_of(rng, extent, shards, -0.22, 0.18)
    return jnp.clip(drawn, -bound, bound).astype(held_as)


def setup_inputs(seed: int = 0) -> dict:
    key_list = jax.random.split(jax.random.key(seed), 8)
    volume = jnp.clip(2.0 * jax.random.uniform(key_list[0], (NBLOCKS, BZ, YW, VX), jnp.float32) ** level_of(key_list[0], (NBLOCKS, BZ, YW, VX), ((0, 512),), -0.2, 0.2), 0.0, 2.0)
    footprint = normal_values(key_list[1], (ANGLES, YW, VX, DC), (YW * VX) ** -0.5, 0.1875, ((0, 512),))
    measured = jnp.clip(3.0 * jax.random.uniform(key_list[2], (VIEWS, DR, DC), jnp.float32) ** level_of(key_list[2], (VIEWS, DR, DC), ((0, 512),), -0.2, 0.2), 0.0, 3.0).astype(jnp.bfloat16)
    angle_index = plant(jax.random.randint(key_list[3], (VIEWS,), 0, A_DEV), jax.random.fold_in(key_list[3], 1), 0, A_DEV - 1).astype(jnp.int32)
    cover = draw_cover(jax.random.fold_in(key_list[7], 71), 0)
    offset = plant(jax.random.randint(key_list[5], (VIEWS, KMAX), 0, DR - BZ + 1), jax.random.fold_in(key_list[5], 1), 0, DR - BZ).astype(jnp.int32)
    count = plant(jax.random.randint(key_list[6], (VIEWS,), 1, KMAX + 1), jax.random.fold_in(key_list[6], 1), 1, KMAX).astype(jnp.int32)
    return {"volume": volume, "footprint": footprint, "measured": measured, "angle_index": angle_index, "cover": cover, "offset": offset, "count": count}


DELTA = 0.5
PRIOR_WEIGHT = 2.0


def reference(volume, footprint, measured, angle_index, cover, offset, count):
    vol_bf = volume.astype(jnp.bfloat16)
    nviews = measured.shape[0]
    zero_index = jnp.zeros((), jnp.int32)

    def view_step(grad, input_arrays):
        view_number, gantry_angle, block_indices, start_offsets, active_count, measured_sinogram = input_arrays
        table_row = footprint[(view_number // V_DEV) * A_DEV + gantry_angle].reshape(YW * VX, DC)
        blocks = vol_bf[block_indices].reshape(KMAX * BZ, YW * VX)
        part = jnp.dot(blocks, table_row, preferred_element_type=jnp.float32)
        forward_projection = jnp.zeros((DR, DC), jnp.float32)
        for slot in range(KMAX):
            alive = (slot < active_count).astype(jnp.float32)
            placed = lax.dynamic_update_slice(jnp.zeros((DR, DC), jnp.float32), part[slot * BZ:(slot + 1) * BZ], (start_offsets[slot].astype(jnp.int32), zero_index))
            forward_projection = forward_projection + alive * placed
        measured_float = measured_sinogram.astype(jnp.float32)
        weighted_residual = (jnp.exp(-measured_float) * (forward_projection - measured_float)).astype(jnp.bfloat16)
        for slot in range(KMAX):
            alive = (slot < active_count).astype(jnp.float32)
            picked = lax.dynamic_slice(weighted_residual, (start_offsets[slot].astype(jnp.int32), zero_index), (BZ, DC))
            back = lax.dot_general(picked, table_row, (((1,), (1,)), ((), ())), preferred_element_type=jnp.float32)
            grad = grad.at[block_indices[slot]].add(alive * back.reshape(BZ, YW, VX))
        return grad, None

    views_iota = jnp.arange(nviews, dtype=jnp.int32)
    data_grad, _ = lax.scan(view_step, jnp.zeros(volume.shape, jnp.float32), (views_iota, angle_index, cover, offset, count, measured))

    flat = volume.reshape(NBLOCKS * BZ, YW, VX)
    zdiff = jnp.clip(flat[1:] - flat[:-1], -DELTA, DELTA)
    prior = jnp.zeros(flat.shape, jnp.float32)
    prior = prior.at[1:].add(zdiff).at[:-1].add(-zdiff)
    ydiff = jnp.clip(flat[:, 1:] - flat[:, :-1], -DELTA, DELTA)
    prior = prior.at[:, 1:].add(ydiff).at[:, :-1].add(-ydiff)
    xdiff = jnp.clip(flat[:, :, 1:] - flat[:, :, :-1], -DELTA, DELTA)
    prior = prior.at[:, :, 1:].add(xdiff).at[:, :, :-1].add(-xdiff)
    return data_grad + PRIOR_WEIGHT * prior.reshape(volume.shape)
```

```python
import jax
import jax.numpy as jnp
from jax import lax
from jax.experimental import pallas as pl
from jax.experimental.pallas import tpu as pltpu
from jax.sharding import PartitionSpec as P

DELTA = 0.5
PRIOR_WEIGHT = 2.0
MESH = pl.DeviceIdType.MESH
HOPS = (-2, 2, -1, 1)
BACK = (1, 0, 3, 2)
CORES = 2
NT = (((1,), (1,)), ((), ()))


def chunks(total, width):
    return [(at, min(width, total - at)) for at in range(0, total, width)]


def kernel(
    n_grp,
    n_view,
    angle_ref,
    cover_ref,
    offset_ref,
    count_ref,
    vol_ref,
    fp_hbm,
    meas_hbm,
    out_ref,
    fp,
    meas,
    gain,
    win,
    edge,
    halo,
    sel,
    sel_t,
    hi,
    lo,
    proj,
    wres,
    gsum,
    gwin,
    from_partner,
    out_bf,
    arrived,
    load_sem,
    vol_send,
    vol_recv,
    pass_send,
    pass_recv,
    edge_send,
    edge_recv,
    pg_send,
    pg_recv,
    og_send,
    og_recv,
):
    n_dev = n_grp * n_view
    n_chip = n_dev // CORES
    me = lax.axis_index("grp") * n_view + lax.axis_index("view")
    chip = me // CORES
    core = me % CORES
    tables, plane, channels = fp.shape
    views = angle_ref.shape[0]
    slots = cover_ref.shape[0]
    rows = vol_ref.shape[0]
    slab = rows // 2
    det = meas.shape[0] // views
    chip_rows = CORES * rows
    far_rows = 2 * chip_rows
    rest_rows = 3 * chip_rows
    total_rows = tables * (far_rows + rest_rows)
    far_all = tables * far_rows

    def at(device):
        return (device // n_view, device % n_view)

    def exists(hop):
        return jnp.logical_and(chip + hop >= 0, chip + hop < n_chip)

    def peer(hop):
        return at(jnp.clip(me + CORES * hop, 0, n_dev - 1))

    partner = at(me + 1 - 2 * core)
    below, above = me - 1, me + 1
    has_below, has_above = below >= 0, above < n_dev

    loads = [pltpu.make_async_copy(fp_hbm, fp, load_sem.at[0]), pltpu.make_async_copy(meas_hbm, meas, load_sem.at[1])]
    for copy in loads:
        copy.start()

    for j, hop in enumerate(HOPS):

        @pl.when(jnp.logical_not(exists(hop)))
        def _(j=j):
            win[2 * j] = jnp.zeros_like(win[2 * j])
            win[2 * j + 1] = jnp.zeros_like(win[2 * j + 1])
            arrived[j] = jnp.zeros_like(arrived[j])

    @pl.when(jnp.logical_not(has_below))
    def _():
        halo[0] = jnp.zeros_like(halo[0])

    @pl.when(jnp.logical_not(has_above))
    def _():
        halo[1] = jnp.zeros_like(halo[1])

    win[8 + core] = vol_ref[...].astype(jnp.bfloat16)
    edge[0] = vol_ref[0:1, :]
    edge[1] = vol_ref[rows - 1 : rows, :]

    barrier = pltpu.get_barrier_semaphore()
    pl.semaphore_signal(barrier, inc=1, device_id=partner, device_id_type=MESH)
    expected = jnp.int32(1)
    for hop in HOPS:

        @pl.when(exists(hop))
        def _(hop=hop):
            pl.semaphore_signal(barrier, inc=1, device_id=peer(hop), device_id_type=MESH)

        expected = expected + exists(hop).astype(jnp.int32)
    across = jnp.where(core == 0, below, above)
    has_across = jnp.logical_and(across >= 0, across < n_dev)

    @pl.when(has_across)
    def _():
        pl.semaphore_signal(barrier, inc=1, device_id=at(across), device_id_type=MESH)

    expected = expected + has_across.astype(jnp.int32)
    pl.semaphore_wait(barrier, expected)

    vol_copies = [
        pltpu.make_async_remote_copy(
            src_ref=win.at[8 + core],
            dst_ref=win.at[2 * BACK[j] + core],
            send_sem=vol_send.at[j],
            recv_sem=vol_recv.at[BACK[j]],
            device_id=peer(hop),
            device_id_type=MESH,
        )
        for j, hop in enumerate(HOPS)
    ]
    pass_copies = [
        pltpu.make_async_remote_copy(
            src_ref=win.at[2 * j + core],
            dst_ref=win.at[2 * j + core],
            send_sem=pass_send.at[j],
            recv_sem=pass_recv.at[j],
            device_id=partner,
            device_id_type=MESH,
        )
        for j in range(5)
    ]
    edge_copies = [
        pltpu.make_async_remote_copy(
            src_ref=edge.at[side],
            dst_ref=halo.at[1 - side],
            send_sem=edge_send.at[side],
            recv_sem=edge_recv.at[1 - side],
            device_id=at(jnp.clip(target, 0, n_dev - 1)),
            device_id_type=MESH,
        )
        for side, target in enumerate((below, above))
    ]
    for j, hop in enumerate(HOPS):

        @pl.when(exists(hop))
        def _(j=j):
            vol_copies[j].start()

    pass_copies[4].start()

    @pl.when(has_below)
    def _():
        edge_copies[0].start()

    @pl.when(has_above)
    def _():
        edge_copies[1].start()

    first_block = (chip - 2) * 4
    row_of = []
    for v in range(views):
        here = []
        for k in range(slots):
            block = cover_ref[k, v] - first_block
            chip_at = block // 4
            place = 4 - 2 * jnp.abs(chip_at - 2) + jnp.where(chip_at > 2, 1, 0)
            inside = place * chip_rows + (block % 4) * slab
            table = angle_ref[v]
            row = jnp.where(
                place < 2,
                table * far_rows + inside,
                far_all + table * rest_rows + inside - far_rows,
            )
            row = row - offset_ref[k, v]
            here.append((row, offset_ref[k, v], k < count_ref[v]))
        row_of.append(here)

    det_iota = lax.broadcasted_iota(jnp.int32, (det, 128), 0)
    for v in range(views):
        goals = []
        for row, off, live in row_of[v]:
            off_live = jnp.where(live, off, -4096)
            inside = jnp.logical_and(det_iota >= off_live, det_iota < off_live + slab)
            goals.append(jnp.where(inside, det_iota + row, -1))
        for tile in range(total_rows // 128):
            lane = lax.broadcasted_iota(jnp.int32, (det, 128), 1) + tile * 128
            hits = jnp.zeros((det, 128), jnp.float32)
            for goal in goals:
                hits = hits + jnp.where(goal == lane, 1.0, 0.0)
            sel_t[pl.ds(v * det, det), pl.ds(tile * 128, 128)] = hits.astype(jnp.bfloat16)
    lane = lax.broadcasted_iota(jnp.int32, (8, views * det), 1)
    goals = []
    for k in range(slots):
        goal = jnp.full((8, views * det), -1, jnp.int32)
        for v in range(views):
            row, off, live = row_of[v][k]
            off_live = jnp.where(live, off, -4096)
            spot = lane - v * det
            inside = jnp.logical_and(
                jnp.logical_and(spot >= off_live, spot < off_live + slab),
                jnp.logical_and(spot >= 0, spot < det),
            )
            goal = jnp.where(inside, spot + row, goal)
        goals.append(goal[0:1, :])

    def build_sel(step, _):
        at_row = pl.multiple_of(step * 32, 32)
        index = lax.broadcasted_iota(jnp.int32, (32, views * det), 0) + step * 32
        hits = jnp.zeros((32, views * det), jnp.float32)
        for goal in goals:
            hits = hits + jnp.where(goal == index, 1.0, 0.0)
        sel[pl.ds(at_row, 32), :] = hits.astype(jnp.bfloat16)
        return 0

    lax.fori_loop(0, total_rows // 32, build_sel, 0)

    loads[1].wait()

    def build_gain(step, _):
        part = pl.ds(pl.multiple_of(step * 32, 32), 32)
        gain[part, :] = jnp.exp(-meas[part, :].astype(jnp.float32))
        return 0

    lax.fori_loop(0, meas.shape[0] // 32, build_gain, 0)
    loads[0].wait()

    def project(first_slot, slot_count, first_row):
        block = win[pl.ds(first_slot, slot_count)].reshape(slot_count * rows, plane)
        height = slot_count * rows
        for table in range(tables):
            for start, width in chunks(channels, 256):
                cols = pl.ds(start, width)
                product = jnp.dot(block, fp[table, :, cols], preferred_element_type=jnp.float32)
                top = product.astype(jnp.bfloat16)
                part = pl.ds(first_row + table * height, height)
                hi[part, cols] = top
                lo[part, cols] = (product - top.astype(jnp.float32)).astype(jnp.bfloat16)

    def placed(first_row, height, cols):
        pick = sel_t[:, pl.ds(first_row, height)]
        part = pl.ds(first_row, height)
        return jnp.dot(pick, hi[part, cols], preferred_element_type=jnp.float32) + jnp.dot(
            pick, lo[part, cols], preferred_element_type=jnp.float32
        )

    def collect(which):
        for j in which:

            @pl.when(exists(HOPS[j]))
            def _(j=j):
                vol_copies[BACK[j]].wait_recv()
                pass_copies[j].start()

        for j in which:

            @pl.when(exists(HOPS[j]))
            def _(j=j):
                pass_copies[j].wait_recv()

    collect((2, 3))
    pass_copies[4].wait_recv()
    project(4, 6, far_all)
    for start, width in chunks(channels, 256):
        cols = pl.ds(start, width)
        proj[:, cols] = placed(far_all, tables * rest_rows, cols)
    collect((0, 1))
    project(0, 4, 0)
    for start, width in chunks(channels, 256):
        cols = pl.ds(start, width)
        forward = proj[:, cols] + placed(0, far_all, cols)
        wres[:, cols] = (gain[:, cols] * (forward - meas[:, cols].astype(jnp.float32))).astype(jnp.bfloat16)

    def gather(first_row, height):
        part = pl.ds(first_row, height)
        for start, width in chunks(channels, 256):
            cols = pl.ds(start, width)
            gsum[part, cols] = jnp.dot(sel[part, :], wres[:, cols], preferred_element_type=jnp.float32).astype(
                jnp.bfloat16
            )

    def backproject(first_row, stride, first_slot, slot_count):
        height = slot_count * rows
        for start, width in chunks(plane, 256):
            total = None
            for table in range(tables):
                term = lax.dot_general(
                    gsum[pl.ds(first_row + table * stride, height), :],
                    fp[table, pl.ds(start, width), :],
                    NT,
                    preferred_element_type=jnp.float32,
                )
                total = term if total is None else total + term
            gwin[pl.ds(first_slot, slot_count), :, pl.ds(start, width)] = total.reshape(slot_count, rows, width)

    pg_copies = [
        pltpu.make_async_remote_copy(
            src_ref=gwin.at[2 * j + 1 - core],
            dst_ref=from_partner.at[j],
            send_sem=pg_send.at[j],
            recv_sem=pg_recv.at[j],
            device_id=partner,
            device_id_type=MESH,
        )
        for j in range(5)
    ]
    og_copies = [
        pltpu.make_async_remote_copy(
            src_ref=out_bf.at[j],
            dst_ref=arrived.at[BACK[j]],
            send_sem=og_send.at[j],
            recv_sem=og_recv.at[BACK[j]],
            device_id=peer(hop),
            device_id_type=MESH,
        )
        for j, hop in enumerate(HOPS)
    ]

    def hand_out(which):
        for j in which:
            pg_copies[j].wait_recv()
            out_bf[j] = (gwin[2 * j + core] + from_partner[j]).astype(jnp.bfloat16)

            @pl.when(exists(HOPS[j]))
            def _(j=j):
                og_copies[j].start()

    gather(0, far_all)
    backproject(0, far_rows, 0, 4)
    pg_copies[0].start()
    pg_copies[1].start()
    gather(far_all, tables * rest_rows)
    hand_out((0, 1))
    backproject(far_all, rest_rows, 4, 6)
    for j in (2, 3, 4):
        pg_copies[j].start()

    @pl.when(has_below)
    def _():
        edge_copies[1].wait_recv()

    @pl.when(has_above)
    def _():
        edge_copies[0].wait_recv()

    here = vol_ref[...]
    row = lax.broadcasted_iota(jnp.int32, here.shape, 0)
    column = lax.broadcasted_iota(jnp.int32, here.shape, 1) % (plane // 2)

    def step_to(other, allowed):
        return jnp.where(allowed, jnp.clip(here - other, -DELTA, DELTA), 0.0)

    lower = jnp.where(row == 0, halo[0], pltpu.roll(here, 1, 0))
    upper = jnp.where(row == rows - 1, halo[1], pltpu.roll(here, rows - 1, 0))
    prior = step_to(lower, row + me > 0)
    prior = prior + step_to(upper, row + (me + 1 - n_dev) < rows - 1)
    prior = prior + jnp.clip(here - pltpu.roll(here, plane // 2, 1), -DELTA, DELTA)
    prior = prior + step_to(pltpu.roll(here, 1, 1), column > 0)
    prior = prior + step_to(pltpu.roll(here, plane - 1, 1), column < plane // 2 - 1)
    out_ref[...] = PRIOR_WEIGHT * prior

    hand_out((2, 3))
    pg_copies[4].wait_recv()
    total = out_ref[...] + gwin[8 + core] + from_partner[4]
    for j in (2, 3, 0, 1):

        @pl.when(exists(HOPS[j]))
        def _(j=j):
            og_copies[BACK[j]].wait_recv()

        total = total + arrived[j].astype(jnp.float32)
    out_ref[...] = total

    for j, hop in enumerate(HOPS):

        @pl.when(exists(hop))
        def _(j=j):
            vol_copies[j].wait_send()
            pass_copies[j].wait_send()
            og_copies[j].wait_send()

    pass_copies[4].wait_send()
    for j in range(5):
        pg_copies[j].wait_send()

    @pl.when(has_below)
    def _():
        edge_copies[0].wait_send()

    @pl.when(has_above)
    def _():
        edge_copies[1].wait_send()


def solution(mesh):
    n_grp, n_view = mesh.shape["grp"], mesh.shape["view"]

    def shards(volume, footprint, measured, angle_index, cover, offset, count):
        blocks, slab, strip, width = volume.shape
        views, det, channels = measured.shape
        tables = footprint.shape[0]
        rows, plane = blocks * slab, strip * width
        total_rows = tables * 5 * CORES * rows
        bf, f32 = jnp.bfloat16, jnp.float32
        dma = pltpu.SemaphoreType.DMA
        smem = pl.BlockSpec(memory_space=pltpu.SMEM)
        vmem = pl.BlockSpec(memory_space=pltpu.VMEM)
        hbm = pl.BlockSpec(memory_space=pltpu.HBM)
        gradient = pl.pallas_call(
            lambda *refs: kernel(n_grp, n_view, *refs),
            out_shape=jax.ShapeDtypeStruct((rows, plane), f32),
            in_specs=[smem, smem, smem, smem, vmem, hbm, hbm],
            out_specs=vmem,
            scratch_shapes=[
                pltpu.VMEM((tables, plane, channels), bf),
                pltpu.VMEM((views * det, channels), bf),
                pltpu.VMEM((views * det, channels), f32),
                pltpu.VMEM((10, rows, plane), bf),
                pltpu.VMEM((2, 1, plane), f32),
                pltpu.VMEM((2, 1, plane), f32),
                pltpu.VMEM((total_rows, views * det), bf),
                pltpu.VMEM((views * det, total_rows), bf),
                pltpu.VMEM((total_rows, channels), bf),
                pltpu.VMEM((total_rows, channels), bf),
                pltpu.VMEM((views * det, channels), f32),
                pltpu.VMEM((views * det, channels), bf),
                pltpu.VMEM((total_rows, channels), bf),
                pltpu.VMEM((10, rows, plane), f32),
                pltpu.VMEM((5, rows, plane), f32),
                pltpu.VMEM((4, rows, plane), bf),
                pltpu.VMEM((4, rows, plane), bf),
                dma((2,)),
                dma((4,)),
                dma((4,)),
                dma((5,)),
                dma((5,)),
                dma((2,)),
                dma((2,)),
                dma((5,)),
                dma((5,)),
                dma((4,)),
                dma((4,)),
            ],
            compiler_params=pltpu.CompilerParams(
                collective_id=0, has_side_effects=True, vmem_limit_bytes=67_043_328
            ),
            name="ct_gradient",
        )(
            angle_index,
            cover.T,
            offset.T,
            count,
            volume.reshape(rows, plane),
            footprint.reshape(tables, plane, channels),
            measured.reshape(views * det, channels),
        )
        return gradient.reshape(volume.shape)

    axes = ("grp", "view")
    in_specs = (
        P(axes, None, None, None),
        P(axes, None, None, None),
        P(axes, None, None),
        P(axes),
        P(axes, None),
        P(axes, None),
        P(axes),
    )
    return jax.shard_map(
        shards, mesh=mesh, in_specs=in_specs, out_specs=P(axes, None, None, None), check_vma=False
    )
```

```python
import jax
import jax.numpy as jnp
from jax import lax
from jax.experimental import pallas as pl
from jax.experimental.pallas import tpu as pltpu
from jax.sharding import PartitionSpec as P

DELTA = 0.5
PRIOR_WEIGHT = 2.0
MESH = pl.DeviceIdType.MESH
HOPS = (-2, 2, -1, 1)
BACK = (1, 0, 3, 2)
CORES = 2
NT = (((1,), (1,)), ((), ()))


def chunks(total, width):
    return [(at, min(width, total - at)) for at in range(0, total, width)]


def kernel(
    n_grp,
    n_view,
    angle_hbm,
    cover_hbm,
    offset_hbm,
    count_hbm,
    vol_hbm,
    fp_hbm,
    meas_hbm,
    out_ref,
    angle_ref,
    cover_ref,
    offset_ref,
    count_ref,
    raw,
    vol_ref,
    fp,
    meas,
    gain,
    win,
    edge,
    halo,
    sel,
    sel_t,
    hi,
    lo,
    proj,
    wres,
    gsum,
    gwin,
    from_partner,
    out_bf,
    arrived,
    load_sem,
    vol_send,
    vol_recv,
    pass_send,
    pass_recv,
    edge_send,
    edge_recv,
    pg_send,
    pg_recv,
    og_send,
    og_recv,
):
    n_dev = n_grp * n_view
    n_chip = n_dev // CORES
    me = lax.axis_index("grp") * n_view + lax.axis_index("view")
    chip = me // CORES
    core = me % CORES
    tables, plane, channels = fp.shape
    views = angle_ref.shape[0]
    slots = cover_ref.shape[0]
    rows = vol_ref.shape[0]
    slab = rows // 2
    pieces = plane // 128
    det = meas.shape[0] // views
    chip_rows = CORES * rows
    far_rows = 2 * chip_rows
    rest_rows = 3 * chip_rows
    total_rows = tables * (far_rows + rest_rows)
    far_all = tables * far_rows

    def at(device):
        return (device // n_view, device % n_view)

    def exists(hop):
        return jnp.logical_and(chip + hop >= 0, chip + hop < n_chip)

    def peer(hop):
        return at(jnp.clip(me + CORES * hop, 0, n_dev - 1))

    partner = at(me + 1 - 2 * core)
    below, above = me - 1, me + 1
    has_below, has_above = below >= 0, above < n_dev

    barrier = pltpu.get_barrier_semaphore()
    pl.semaphore_signal(barrier, inc=1, device_id=partner, device_id_type=MESH)
    expected = jnp.int32(1)
    for hop in HOPS:

        @pl.when(exists(hop))
        def _(hop=hop):
            pl.semaphore_signal(barrier, inc=1, device_id=peer(hop), device_id_type=MESH)

        expected = expected + exists(hop).astype(jnp.int32)
    across = jnp.where(core == 0, below, above)
    has_across = jnp.logical_and(across >= 0, across < n_dev)

    @pl.when(has_across)
    def _():
        pl.semaphore_signal(barrier, inc=1, device_id=at(across), device_id_type=MESH)

    expected = expected + has_across.astype(jnp.int32)

    loads = [
        pltpu.make_async_copy(source, target, load_sem.at[n])
        for n, (source, target) in enumerate(
            (
                (vol_hbm, raw),
                (angle_hbm, angle_ref),
                (cover_hbm, cover_ref),
                (offset_hbm, offset_ref),
                (count_hbm, count_ref),
                (meas_hbm, meas),
                (fp_hbm, fp),
            )
        )
    ]
    for copy in loads:
        copy.start()
    loads[0].wait()
    for piece in range(pieces):
        at_column = ((piece % 2) * (pieces // 2) + piece // 2) * 128
        value = raw[pl.ds(piece, rows, stride=pieces), :]
        vol_ref[:, pl.ds(at_column, 128)] = value
        win[8 + core, :, pl.ds(at_column, 128)] = value.astype(jnp.bfloat16)
    edge[0] = vol_ref[0:1, :]
    edge[1] = vol_ref[rows - 1 : rows, :]

    for j, hop in enumerate(HOPS):

        @pl.when(jnp.logical_not(exists(hop)))
        def _(j=j):
            win[2 * j] = jnp.zeros_like(win[2 * j])
            win[2 * j + 1] = jnp.zeros_like(win[2 * j + 1])
            arrived[j] = jnp.zeros_like(arrived[j])

    @pl.when(jnp.logical_not(has_below))
    def _():
        halo[0] = jnp.zeros_like(halo[0])

    @pl.when(jnp.logical_not(has_above))
    def _():
        halo[1] = jnp.zeros_like(halo[1])

    pl.semaphore_wait(barrier, expected)

    vol_copies = [
        pltpu.make_async_remote_copy(
            src_ref=win.at[8 + core],
            dst_ref=win.at[2 * BACK[j] + core],
            send_sem=vol_send.at[j],
            recv_sem=vol_recv.at[BACK[j]],
            device_id=peer(hop),
            device_id_type=MESH,
        )
        for j, hop in enumerate(HOPS)
    ]
    pass_copies = [
        pltpu.make_async_remote_copy(
            src_ref=win.at[2 * j + core],
            dst_ref=win.at[2 * j + core],
            send_sem=pass_send.at[j],
            recv_sem=pass_recv.at[j],
            device_id=partner,
            device_id_type=MESH,
        )
        for j in range(5)
    ]
    edge_copies = [
        pltpu.make_async_remote_copy(
            src_ref=edge.at[side],
            dst_ref=halo.at[1 - side],
            send_sem=edge_send.at[side],
            recv_sem=edge_recv.at[1 - side],
            device_id=at(jnp.clip(target, 0, n_dev - 1)),
            device_id_type=MESH,
        )
        for side, target in enumerate((below, above))
    ]
    for j in (2, 3, 0, 1):

        @pl.when(exists(HOPS[j]))
        def _(j=j):
            vol_copies[j].start()

    pass_copies[4].start()

    @pl.when(has_below)
    def _():
        edge_copies[0].start()

    @pl.when(has_above)
    def _():
        edge_copies[1].start()

    for copy in loads[1:5]:
        copy.wait()

    first_block = (chip - 2) * 4
    row_of = []
    for v in range(views):
        here = []
        for k in range(slots):
            block = cover_ref[k, v] - first_block
            chip_at = block // 4
            place = 4 - 2 * jnp.abs(chip_at - 2) + jnp.where(chip_at > 2, 1, 0)
            inside = place * chip_rows + (block % 4) * slab
            table = angle_ref[v]
            row = jnp.where(
                place < 2,
                table * far_rows + inside,
                far_all + table * rest_rows + inside - far_rows,
            )
            row = row - offset_ref[k, v]
            here.append((row, offset_ref[k, v], k < count_ref[v]))
        row_of.append(here)

    det_iota = lax.broadcasted_iota(jnp.int32, (det, 128), 0)
    for v in range(views):
        goals = []
        for row, off, live in row_of[v]:
            off_live = jnp.where(live, off, -4096)
            inside = jnp.logical_and(det_iota >= off_live, det_iota < off_live + slab)
            goals.append(jnp.where(inside, det_iota + row, -1))
        for tile in range(total_rows // 128):
            lane = lax.broadcasted_iota(jnp.int32, (det, 128), 1) + tile * 128
            hits = jnp.zeros((det, 128), jnp.float32)
            for goal in goals:
                hits = hits + jnp.where(goal == lane, 1.0, 0.0)
            sel_t[pl.ds(v * det, det), pl.ds(tile * 128, 128)] = hits.astype(jnp.bfloat16)
    lane = lax.broadcasted_iota(jnp.int32, (8, views * det), 1)
    goals = []
    for k in range(slots):
        goal = jnp.full((8, views * det), -1, jnp.int32)
        for v in range(views):
            row, off, live = row_of[v][k]
            off_live = jnp.where(live, off, -4096)
            spot = lane - v * det
            inside = jnp.logical_and(
                jnp.logical_and(spot >= off_live, spot < off_live + slab),
                jnp.logical_and(spot >= 0, spot < det),
            )
            goal = jnp.where(inside, spot + row, goal)
        goals.append(goal[0:1, :])

    def build_sel(step, _):
        at_row = pl.multiple_of(step * 32, 32)
        index = lax.broadcasted_iota(jnp.int32, (32, views * det), 0) + step * 32
        hits = jnp.zeros((32, views * det), jnp.float32)
        for goal in goals:
            hits = hits + jnp.where(goal == index, 1.0, 0.0)
        sel[pl.ds(at_row, 32), :] = hits.astype(jnp.bfloat16)
        return 0

    lax.fori_loop(0, total_rows // 32, build_sel, 0)

    loads[5].wait()

    def build_gain(step, _):
        part = pl.ds(pl.multiple_of(step * 32, 32), 32)
        gain[part, :] = jnp.exp(-meas[part, :].astype(jnp.float32))
        return 0

    lax.fori_loop(0, meas.shape[0] // 32, build_gain, 0)
    loads[6].wait()

    def project(first_slot, slot_count, first_row):
        block = win[pl.ds(first_slot, slot_count)].reshape(slot_count * rows, plane)
        height = slot_count * rows
        for table in range(tables):
            for start, width in chunks(channels, 256):
                cols = pl.ds(start, width)
                product = jnp.dot(block, fp[table, :, cols], preferred_element_type=jnp.float32)
                top = product.astype(jnp.bfloat16)
                part = pl.ds(first_row + table * height, height)
                hi[part, cols] = top
                lo[part, cols] = (product - top.astype(jnp.float32)).astype(jnp.bfloat16)

    def placed(first_row, height, cols):
        pick = sel_t[:, pl.ds(first_row, height)]
        part = pl.ds(first_row, height)
        return jnp.dot(pick, hi[part, cols], preferred_element_type=jnp.float32) + jnp.dot(
            pick, lo[part, cols], preferred_element_type=jnp.float32
        )

    def collect(which):
        for j in which:

            @pl.when(exists(HOPS[j]))
            def _(j=j):
                vol_copies[BACK[j]].wait_recv()
                pass_copies[j].start()

        for j in which:

            @pl.when(exists(HOPS[j]))
            def _(j=j):
                pass_copies[j].wait_recv()

    collect((2, 3))
    pass_copies[4].wait_recv()
    project(4, 6, far_all)
    for start, width in chunks(channels, 256):
        cols = pl.ds(start, width)
        proj[:, cols] = placed(far_all, tables * rest_rows, cols)
    collect((0, 1))
    project(0, 4, 0)
    for start, width in chunks(channels, 256):
        cols = pl.ds(start, width)
        forward = proj[:, cols] + placed(0, far_all, cols)
        wres[:, cols] = (gain[:, cols] * (forward - meas[:, cols].astype(jnp.float32))).astype(jnp.bfloat16)

    def gather(first_row, height):
        part = pl.ds(first_row, height)
        for start, width in chunks(channels, 256):
            cols = pl.ds(start, width)
            gsum[part, cols] = jnp.dot(sel[part, :], wres[:, cols], preferred_element_type=jnp.float32).astype(
                jnp.bfloat16
            )

    def backproject(first_row, stride, first_slot, slot_count):
        height = slot_count * rows
        for start, width in chunks(plane, 256):
            total = None
            for table in range(tables):
                term = lax.dot_general(
                    gsum[pl.ds(first_row + table * stride, height), :],
                    fp[table, pl.ds(start, width), :],
                    NT,
                    preferred_element_type=jnp.float32,
                )
                total = term if total is None else total + term
            gwin[pl.ds(first_slot, slot_count), :, pl.ds(start, width)] = total.reshape(slot_count, rows, width)

    pg_copies = [
        pltpu.make_async_remote_copy(
            src_ref=gwin.at[2 * j + 1 - core],
            dst_ref=from_partner.at[j],
            send_sem=pg_send.at[j],
            recv_sem=pg_recv.at[j],
            device_id=partner,
            device_id_type=MESH,
        )
        for j in range(5)
    ]
    og_copies = [
        pltpu.make_async_remote_copy(
            src_ref=out_bf.at[j],
            dst_ref=arrived.at[BACK[j]],
            send_sem=og_send.at[j],
            recv_sem=og_recv.at[BACK[j]],
            device_id=peer(hop),
            device_id_type=MESH,
        )
        for j, hop in enumerate(HOPS)
    ]

    def hand_out(which):
        for j in which:
            pg_copies[j].wait_recv()
            out_bf[j] = (gwin[2 * j + core] + from_partner[j]).astype(jnp.bfloat16)

            @pl.when(exists(HOPS[j]))
            def _(j=j):
                og_copies[j].start()

    gather(0, far_all)
    backproject(0, far_rows, 0, 4)
    pg_copies[0].start()
    pg_copies[1].start()
    gather(far_all, tables * rest_rows)
    hand_out((0, 1))
    backproject(far_all, rest_rows, 4, 6)
    for j in (2, 3, 4):
        pg_copies[j].start()

    @pl.when(has_below)
    def _():
        edge_copies[1].wait_recv()

    @pl.when(has_above)
    def _():
        edge_copies[0].wait_recv()

    here = vol_ref[...]
    row = lax.broadcasted_iota(jnp.int32, here.shape, 0)
    column = lax.broadcasted_iota(jnp.int32, here.shape, 1) % (plane // 2)

    def step_to(other, allowed):
        return jnp.where(allowed, jnp.clip(here - other, -DELTA, DELTA), 0.0)

    lower = jnp.where(row == 0, halo[0], pltpu.roll(here, 1, 0))
    upper = jnp.where(row == rows - 1, halo[1], pltpu.roll(here, rows - 1, 0))
    prior = step_to(lower, row + me > 0)
    prior = prior + step_to(upper, row + (me + 1 - n_dev) < rows - 1)
    prior = prior + jnp.clip(here - pltpu.roll(here, plane // 2, 1), -DELTA, DELTA)
    prior = prior + step_to(pltpu.roll(here, 1, 1), column > 0)
    prior = prior + step_to(pltpu.roll(here, plane - 1, 1), column < plane // 2 - 1)
    vol_ref[...] = PRIOR_WEIGHT * prior

    hand_out((2, 3))
    pg_copies[4].wait_recv()
    total = vol_ref[...] + gwin[8 + core] + from_partner[4]
    for j in (2, 3, 0, 1):

        @pl.when(exists(HOPS[j]))
        def _(j=j):
            og_copies[BACK[j]].wait_recv()

        total = total + arrived[j].astype(jnp.float32)
    for piece in range(pieces):
        at_column = ((piece % 2) * (pieces // 2) + piece // 2) * 128
        out_ref[pl.ds(piece, rows, stride=pieces), :] = total[:, at_column : at_column + 128]

    for j, hop in enumerate(HOPS):

        @pl.when(exists(hop))
        def _(j=j):
            vol_copies[j].wait_send()
            pass_copies[j].wait_send()
            og_copies[j].wait_send()

    pass_copies[4].wait_send()
    for j in range(5):
        pg_copies[j].wait_send()

    @pl.when(has_below)
    def _():
        edge_copies[0].wait_send()

    @pl.when(has_above)
    def _():
        edge_copies[1].wait_send()


def solution(mesh):
    n_grp, n_view = mesh.shape["grp"], mesh.shape["view"]

    def shards(volume, footprint, measured, angle_index, cover, offset, count):
        blocks, slab, strip, width = volume.shape
        views, det, channels = measured.shape
        tables = footprint.shape[0]
        rows, plane = blocks * slab, strip * width
        total_rows = tables * 5 * CORES * rows
        bf, f32 = jnp.bfloat16, jnp.float32
        dma = pltpu.SemaphoreType.DMA
        vmem = pl.BlockSpec(memory_space=pltpu.VMEM)
        hbm = pl.BlockSpec(memory_space=pltpu.HBM)
        gradient = pl.pallas_call(
            lambda *refs: kernel(n_grp, n_view, *refs),
            out_shape=jax.ShapeDtypeStruct((rows * plane // 128, 128), f32),
            in_specs=[hbm] * 7,
            out_specs=vmem,
            scratch_shapes=[
                pltpu.SMEM(angle_index.shape, jnp.int32),
                pltpu.SMEM(cover.T.shape, jnp.int32),
                pltpu.SMEM(offset.T.shape, jnp.int32),
                pltpu.SMEM(count.shape, jnp.int32),
                pltpu.VMEM((rows * plane // 128, 128), f32),
                pltpu.VMEM((rows, plane), f32),
                pltpu.VMEM((tables, plane, channels), bf),
                pltpu.VMEM((views * det, channels), bf),
                pltpu.VMEM((views * det, channels), f32),
                pltpu.VMEM((10, rows, plane), bf),
                pltpu.VMEM((2, 1, plane), f32),
                pltpu.VMEM((2, 1, plane), f32),
                pltpu.VMEM((total_rows, views * det), bf),
                pltpu.VMEM((views * det, total_rows), bf),
                pltpu.VMEM((total_rows, channels), bf),
                pltpu.VMEM((total_rows, channels), bf),
                pltpu.VMEM((views * det, channels), f32),
                pltpu.VMEM((views * det, channels), bf),
                pltpu.VMEM((total_rows, channels), bf),
                pltpu.VMEM((10, rows, plane), f32),
                pltpu.VMEM((5, rows, plane), f32),
                pltpu.VMEM((4, rows, plane), bf),
                pltpu.VMEM((4, rows, plane), bf),
                dma((7,)),
                dma((4,)),
                dma((4,)),
                dma((5,)),
                dma((5,)),
                dma((2,)),
                dma((2,)),
                dma((5,)),
                dma((5,)),
                dma((4,)),
                dma((4,)),
            ],
            compiler_params=pltpu.CompilerParams(
                collective_id=0, has_side_effects=True, vmem_limit_bytes=67_043_328
            ),
            name="ct_gradient",
        )(
            angle_index,
            cover.T,
            offset.T,
            count,
            volume.reshape(rows, strip, width // 128, 128).transpose(0, 2, 1, 3).reshape(-1, 128),
            footprint.reshape(tables, plane, channels),
            measured.reshape(views * det, channels),
        )
        return gradient.reshape(rows, width // 128, strip, 128).transpose(0, 2, 1, 3).reshape(volume.shape)

    axes = ("grp", "view")
    in_specs = (
        P(axes, None, None, None),
        P(axes, None, None, None),
        P(axes, None, None),
        P(axes),
        P(axes, None),
        P(axes, None),
        P(axes),
    )
    return jax.shard_map(
        shards, mesh=mesh, in_specs=in_specs, out_specs=P(axes, None, None, None), check_vma=False
    )
```

```python
import jax
import jax.numpy as jnp
from jax import lax
from jax.experimental import pallas as pl
from jax.experimental.pallas import tpu as pltpu
from jax.sharding import PartitionSpec as P

DELTA = 0.5
PRIOR_WEIGHT = 2.0
MESH = pl.DeviceIdType.MESH
HOPS = (1, 2, -1, -2)
BACK = (2, 3, 0, 1)
CORES = 2
LINE = 8
NT = (((1,), (1,)), ((), ()))


def chunks(total, width):
    return [(at, min(width, total - at)) for at in range(0, total, width)]


def kernel(
    n_grp,
    n_view,
    angle_hbm,
    cover_hbm,
    offset_hbm,
    count_hbm,
    vol_hbm,
    fp_hbm,
    meas_hbm,
    out_ref,
    angle_ref,
    cover_ref,
    offset_ref,
    count_ref,
    raw,
    vol_ref,
    fp,
    meas,
    gain,
    win,
    edge,
    halo,
    sel,
    sel_t,
    hi,
    lo,
    proj,
    wres,
    gsum,
    gwin,
    box,
    from_partner,
    out_bf,
    arrived,
    load_sem,
    vol_send,
    vol_recv,
    pass_send,
    pass_recv,
    edge_send,
    edge_recv,
    pg_send,
    pg_recv,
    og_send,
    og_recv,
    box_send,
    box_recv,
    fwd_send,
    here_sem,
):
    n_dev = n_grp * n_view
    n_chip = n_dev // CORES
    me = lax.axis_index("grp") * n_view + lax.axis_index("view")
    chip = me // CORES
    core = me % CORES
    tables, plane, channels = fp.shape
    views = angle_ref.shape[0]
    slots = cover_ref.shape[0]
    rows = vol_ref.shape[0]
    slab = rows // 2
    pieces = plane // 128
    det = meas.shape[0] // views
    chip_rows = CORES * rows
    first_rows, last_rows, hop_rows = 3 * chip_rows, 2 * chip_rows, 4 * chip_rows
    first_all, hop_all = tables * first_rows, tables * hop_rows
    total_rows = tables * 5 * chip_rows
    in_line = chip % LINE
    line = chip // LINE
    span = CORES * LINE
    line_below, line_above = line > 0, line < n_chip // LINE - 1

    def at(device):
        return (device // n_view, device % n_view)

    def exists(hop):
        return jnp.logical_and(chip + hop >= 0, chip + hop < n_chip)

    def peer(hop):
        return at(jnp.clip(me + CORES * hop, 0, n_dev - 1))

    partner = at(me + 1 - 2 * core)
    below, above = me - 1, me + 1
    has_below, has_above = below >= 0, above < n_dev

    def crosses(hop):
        return jnp.logical_or(in_line + hop < 0, in_line + hop >= LINE)

    def direct(hop):
        return jnp.logical_and(exists(hop), jnp.logical_not(crosses(hop))) if hop < 0 else exists(hop)

    relay = jnp.logical_and(in_line < 2, line_above)
    relay_near = jnp.logical_and(in_line == 0, line_above)
    boxed = jnp.logical_and(in_line < 2, line_below)
    tail = jnp.logical_and(in_line >= LINE - 2, line_above)
    tail_last = jnp.logical_and(in_line == LINE - 1, line_above)

    def device_at(offset):
        return at(jnp.clip(me + offset, 0, n_dev - 1))

    barrier = pltpu.get_barrier_semaphore()
    expected = jnp.int32(1)

    def greet(allowed, offset, count=1):
        @pl.when(allowed)
        def _():
            pl.semaphore_signal(barrier, inc=count, device_id=device_at(offset), device_id_type=MESH)

    for hop in HOPS:
        if hop > 0:
            greet(jnp.logical_and(exists(hop), jnp.logical_not(crosses(hop))), CORES * hop)
        else:
            greet(exists(hop), CORES * hop)
        expected = expected + direct(hop).astype(jnp.int32)
    greet(relay, span)
    greet(relay_near, span - CORES)
    greet(relay, span - 2 * CORES)
    expected = expected + boxed.astype(jnp.int32) + tail.astype(jnp.int32) + tail_last.astype(jnp.int32)
    pl.semaphore_signal(barrier, inc=1, device_id=partner, device_id_type=MESH)
    greet(jnp.logical_and(core == 0, has_below), -1)
    greet(jnp.logical_and(core == 1, jnp.logical_and(has_above, in_line < LINE - 1)), 1)
    expected = expected + jnp.logical_and(core == 1, has_above).astype(jnp.int32)
    expected = expected + jnp.logical_and(core == 0, in_line > 0).astype(jnp.int32)

    loads = [
        pltpu.make_async_copy(source, target, load_sem.at[n])
        for n, (source, target) in enumerate(
            (
                (vol_hbm, raw),
                (angle_hbm, angle_ref),
                (cover_hbm, cover_ref),
                (offset_hbm, offset_ref),
                (count_hbm, count_ref),
                (meas_hbm, meas),
                (fp_hbm, fp),
            )
        )
    ]
    for copy in loads:
        copy.start()
    loads[0].wait()
    for piece in range(pieces):
        at_column = ((piece % 2) * (pieces // 2) + piece // 2) * 128
        value = raw[pl.ds(piece, rows, stride=pieces), :]
        vol_ref[:, pl.ds(at_column, 128)] = value
        win[core, :, pl.ds(at_column, 128)] = value.astype(jnp.bfloat16)
    edge[0] = vol_ref[0:1, :]
    edge[1] = vol_ref[rows - 1 : rows, :]

    for j, hop in enumerate(HOPS):

        @pl.when(jnp.logical_not(exists(hop)))
        def _(j=j):
            win[2 + 2 * j] = jnp.zeros_like(win[2 + 2 * j])
            win[3 + 2 * j] = jnp.zeros_like(win[3 + 2 * j])
            arrived[j] = jnp.zeros_like(arrived[j])

    @pl.when(jnp.logical_not(has_below))
    def _():
        halo[0] = jnp.zeros_like(halo[0])

    @pl.when(jnp.logical_not(has_above))
    def _():
        halo[1] = jnp.zeros_like(halo[1])

    pl.semaphore_wait(barrier, expected)

    def say(allowed, which, offset):
        @pl.when(allowed)
        def _():
            pl.semaphore_signal(here_sem.at[which], inc=1, device_id=device_at(offset), device_id_type=MESH)

    say(tail_last, 0, CORES - span)
    say(tail, 1, 2 * CORES - span)

    vol_copies = [
        pltpu.make_async_remote_copy(
            src_ref=win.at[core],
            dst_ref=win.at[2 + 2 * BACK[j] + core],
            send_sem=vol_send.at[j],
            recv_sem=vol_recv.at[BACK[j]],
            device_id=peer(hop),
            device_id_type=MESH,
        )
        for j, hop in enumerate(HOPS)
    ]
    box_copy = pltpu.make_async_remote_copy(
        src_ref=win.at[core],
        dst_ref=box,
        send_sem=box_send.at[0],
        recv_sem=box_recv.at[0],
        device_id=device_at(-span),
        device_id_type=MESH,
    )
    fwd_copies = [
        pltpu.make_async_remote_copy(
            src_ref=box,
            dst_ref=win.at[2 + 2 * j + core],
            send_sem=fwd_send.at[j],
            recv_sem=vol_recv.at[j],
            device_id=device_at(span - CORES * (j + 1)),
            device_id_type=MESH,
        )
        for j in range(2)
    ]
    window_slot = [2 + 2 * j for j in range(4)] + [0]
    pass_copies = [
        pltpu.make_async_remote_copy(
            src_ref=win.at[slot + core],
            dst_ref=win.at[slot + core],
            send_sem=pass_send.at[j],
            recv_sem=pass_recv.at[j],
            device_id=partner,
            device_id_type=MESH,
        )
        for j, slot in enumerate(window_slot)
    ]
    edge_copies = [
        pltpu.make_async_remote_copy(
            src_ref=edge.at[side],
            dst_ref=halo.at[1 - side],
            send_sem=edge_send.at[side],
            recv_sem=edge_recv.at[1 - side],
            device_id=device_at(2 * side - 1),
            device_id_type=MESH,
        )
        for side in range(2)
    ]

    @pl.when(boxed)
    def _():
        box_copy.start()

    for j in (0, 2, 1, 3):

        @pl.when(direct(HOPS[j]))
        def _(j=j):
            vol_copies[j].start()

    pass_copies[4].start()
    edge_waits = jnp.logical_and(core == 0, in_line == 0)

    @pl.when(jnp.logical_and(has_below, jnp.logical_not(edge_waits)))
    def _():
        edge_copies[0].start()

    @pl.when(has_above)
    def _():
        edge_copies[1].start()

    for copy in loads[1:5]:
        copy.wait()

    first_block = (chip - 2) * 4
    row_of = []
    for v in range(views):
        here = []
        for k in range(slots):
            block = cover_ref[k, v] - first_block
            distance = block // 4 - 2
            place = jnp.where(distance >= 0, distance, 2 - distance)
            inside = place * chip_rows + (block % 4) * slab
            table = angle_ref[v]
            off = offset_ref[k, v]
            ahead = jnp.where(
                place < 3, table * first_rows + inside, first_all + table * last_rows + inside - first_rows
            )
            behind = jnp.where(
                place > 0, table * hop_rows + inside - chip_rows, hop_all + table * chip_rows + inside
            )
            here.append((ahead - off, behind - off, off, k < count_ref[v]))
        row_of.append(here)

    det_iota = lax.broadcasted_iota(jnp.int32, (det, 128), 0)
    for v in range(views):
        goals = []
        for row, _, off, live in row_of[v]:
            off_live = jnp.where(live, off, -4096)
            inside = jnp.logical_and(det_iota >= off_live, det_iota < off_live + slab)
            goals.append(jnp.where(inside, det_iota + row, -1))
        for tile in range(total_rows // 128):
            lane = lax.broadcasted_iota(jnp.int32, (det, 128), 1) + tile * 128
            hits = jnp.zeros((det, 128), jnp.float32)
            for goal in goals:
                hits = hits + jnp.where(goal == lane, 1.0, 0.0)
            sel_t[pl.ds(v * det, det), pl.ds(tile * 128, 128)] = hits.astype(jnp.bfloat16)
    lane = lax.broadcasted_iota(jnp.int32, (8, views * det), 1)
    goals = []
    for k in range(slots):
        goal = jnp.full((8, views * det), -1, jnp.int32)
        for v in range(views):
            _, row, off, live = row_of[v][k]
            off_live = jnp.where(live, off, -4096)
            spot = lane - v * det
            inside = jnp.logical_and(
                jnp.logical_and(spot >= off_live, spot < off_live + slab),
                jnp.logical_and(spot >= 0, spot < det),
            )
            goal = jnp.where(inside, spot + row, goal)
        goals.append(goal[0:1, :])

    def build_sel(step, _):
        at_row = pl.multiple_of(step * 32, 32)
        index = lax.broadcasted_iota(jnp.int32, (32, views * det), 0) + step * 32
        hits = jnp.zeros((32, views * det), jnp.float32)
        for goal in goals:
            hits = hits + jnp.where(goal == index, 1.0, 0.0)
        sel[pl.ds(at_row, 32), :] = hits.astype(jnp.bfloat16)
        return 0

    lax.fori_loop(0, total_rows // 32, build_sel, 0)

    loads[5].wait()

    def build_gain(step, _):
        part = pl.ds(pl.multiple_of(step * 32, 32), 32)
        gain[part, :] = jnp.exp(-meas[part, :].astype(jnp.float32))
        return 0

    lax.fori_loop(0, meas.shape[0] // 32, build_gain, 0)
    loads[6].wait()

    def project(first_slot, slot_count, first_row):
        block = win[pl.ds(first_slot, slot_count)].reshape(slot_count * rows, plane)
        height = slot_count * rows
        for table in range(tables):
            for start, width in chunks(channels, 256):
                cols = pl.ds(start, width)
                product = jnp.dot(block, fp[table, :, cols], preferred_element_type=jnp.float32)
                top = product.astype(jnp.bfloat16)
                part = pl.ds(first_row + table * height, height)
                hi[part, cols] = top
                lo[part, cols] = (product - top.astype(jnp.float32)).astype(jnp.bfloat16)

    def placed(first_row, height, cols):
        pick = sel_t[:, pl.ds(first_row, height)]
        part = pl.ds(first_row, height)
        return jnp.dot(pick, hi[part, cols], preferred_element_type=jnp.float32) + jnp.dot(
            pick, lo[part, cols], preferred_element_type=jnp.float32
        )

    def collect(which):
        for j in which:

            @pl.when(exists(HOPS[j]))
            def _(j=j):
                vol_copies[BACK[j]].wait_recv()
                pass_copies[j].start()

        for j in which:

            @pl.when(exists(HOPS[j]))
            def _(j=j):
                pass_copies[j].wait_recv()

    @pl.when(relay)
    def _():
        box_copy.wait_recv()

    @pl.when(relay_near)
    def _():
        pl.semaphore_wait(here_sem.at[0], 1)
        fwd_copies[0].start()

    @pl.when(relay)
    def _():
        pl.semaphore_wait(here_sem.at[1], 1)
        fwd_copies[1].start()

    pass_copies[4].wait_recv()
    collect((0, 1))
    project(0, 6, 0)
    for start, width in chunks(channels, 256):
        cols = pl.ds(start, width)
        proj[:, cols] = placed(0, first_all, cols)
    collect((2, 3))

    @pl.when(jnp.logical_and(has_below, edge_waits))
    def _():
        edge_copies[0].start()

    project(6, 4, first_all)
    for start, width in chunks(channels, 256):
        cols = pl.ds(start, width)
        forward = proj[:, cols] + placed(first_all, total_rows - first_all, cols)
        wres[:, cols] = (gain[:, cols] * (forward - meas[:, cols].astype(jnp.float32))).astype(jnp.bfloat16)

    def gather(first_row, height):
        part = pl.ds(first_row, height)
        for start, width in chunks(channels, 256):
            cols = pl.ds(start, width)
            gsum[part, cols] = jnp.dot(sel[part, :], wres[:, cols], preferred_element_type=jnp.float32).astype(
                jnp.bfloat16
            )

    def backproject(first_row, stride, first_slot, slot_count):
        height = slot_count * rows
        for start, width in chunks(plane, 256):
            total = None
            for table in range(tables):
                term = lax.dot_general(
                    gsum[pl.ds(first_row + table * stride, height), :],
                    fp[table, pl.ds(start, width), :],
                    NT,
                    preferred_element_type=jnp.float32,
                )
                total = term if total is None else total + term
            gwin[pl.ds(first_slot, slot_count), :, pl.ds(start, width)] = total.reshape(slot_count, rows, width)

    pg_copies = [
        pltpu.make_async_remote_copy(
            src_ref=gwin.at[slot + 1 - core],
            dst_ref=from_partner.at[j],
            send_sem=pg_send.at[j],
            recv_sem=pg_recv.at[j],
            device_id=partner,
            device_id_type=MESH,
        )
        for j, slot in enumerate(window_slot)
    ]
    og_copies = [
        pltpu.make_async_remote_copy(
            src_ref=out_bf.at[j],
            dst_ref=arrived.at[BACK[j]],
            send_sem=og_send.at[j],
            recv_sem=og_recv.at[BACK[j]],
            device_id=peer(hop),
            device_id_type=MESH,
        )
        for j, hop in enumerate(HOPS)
    ]

    def hand_out(which):
        for j in which:
            pg_copies[j].wait_recv()
            out_bf[j] = (gwin[2 + 2 * j + core] + from_partner[j]).astype(jnp.bfloat16)

            @pl.when(exists(HOPS[j]))
            def _(j=j):
                og_copies[j].start()

    gather(0, hop_all)
    backproject(0, hop_rows, 2, 8)
    for j in (0, 2, 1, 3):
        pg_copies[j].start()
    gather(hop_all, total_rows - hop_all)
    hand_out((0, 2, 1, 3))
    backproject(hop_all, chip_rows, 0, 2)
    pg_copies[4].start()

    @pl.when(has_below)
    def _():
        edge_copies[1].wait_recv()

    @pl.when(has_above)
    def _():
        edge_copies[0].wait_recv()

    here = vol_ref[...]
    row = lax.broadcasted_iota(jnp.int32, here.shape, 0)
    column = lax.broadcasted_iota(jnp.int32, here.shape, 1) % (plane // 2)

    def step_to(other, allowed):
        return jnp.where(allowed, jnp.clip(here - other, -DELTA, DELTA), 0.0)

    lower = jnp.where(row == 0, halo[0], pltpu.roll(here, 1, 0))
    upper = jnp.where(row == rows - 1, halo[1], pltpu.roll(here, rows - 1, 0))
    prior = step_to(lower, row + me > 0)
    prior = prior + step_to(upper, row + (me + 1 - n_dev) < rows - 1)
    prior = prior + jnp.clip(here - pltpu.roll(here, plane // 2, 1), -DELTA, DELTA)
    prior = prior + step_to(pltpu.roll(here, 1, 1), column > 0)
    prior = prior + step_to(pltpu.roll(here, plane - 1, 1), column < plane // 2 - 1)
    vol_ref[...] = PRIOR_WEIGHT * prior

    pg_copies[4].wait_recv()
    total = vol_ref[...] + gwin[core] + from_partner[4]
    for j in (0, 1, 2, 3):

        @pl.when(exists(HOPS[j]))
        def _(j=j):
            og_copies[BACK[j]].wait_recv()

        total = total + arrived[j].astype(jnp.float32)
    for piece in range(pieces):
        at_column = ((piece % 2) * (pieces // 2) + piece // 2) * 128
        out_ref[pl.ds(piece, rows, stride=pieces), :] = total[:, at_column : at_column + 128]

    for j, hop in enumerate(HOPS):

        @pl.when(direct(hop))
        def _(j=j):
            vol_copies[j].wait_send()

        @pl.when(exists(hop))
        def _(j=j):
            pass_copies[j].wait_send()
            og_copies[j].wait_send()

    @pl.when(boxed)
    def _():
        box_copy.wait_send()

    @pl.when(relay_near)
    def _():
        fwd_copies[0].wait_send()

    @pl.when(relay)
    def _():
        fwd_copies[1].wait_send()

    pass_copies[4].wait_send()
    for j in range(5):
        pg_copies[j].wait_send()

    @pl.when(has_below)
    def _():
        edge_copies[0].wait_send()

    @pl.when(has_above)
    def _():
        edge_copies[1].wait_send()


def solution(mesh):
    n_grp, n_view = mesh.shape["grp"], mesh.shape["view"]

    def shards(volume, footprint, measured, angle_index, cover, offset, count):
        blocks, slab, strip, width = volume.shape
        views, det, channels = measured.shape
        tables = footprint.shape[0]
        rows, plane = blocks * slab, strip * width
        total_rows = tables * 5 * CORES * rows
        bf, f32 = jnp.bfloat16, jnp.float32
        dma = pltpu.SemaphoreType.DMA
        vmem = pl.BlockSpec(memory_space=pltpu.VMEM)
        hbm = pl.BlockSpec(memory_space=pltpu.HBM)
        gradient = pl.pallas_call(
            lambda *refs: kernel(n_grp, n_view, *refs),
            out_shape=jax.ShapeDtypeStruct((rows * plane // 128, 128), f32),
            in_specs=[hbm] * 7,
            out_specs=vmem,
            scratch_shapes=[
                pltpu.SMEM(angle_index.shape, jnp.int32),
                pltpu.SMEM(cover.T.shape, jnp.int32),
                pltpu.SMEM(offset.T.shape, jnp.int32),
                pltpu.SMEM(count.shape, jnp.int32),
                pltpu.VMEM((rows * plane // 128, 128), f32),
                pltpu.VMEM((rows, plane), f32),
                pltpu.VMEM((tables, plane, channels), bf),
                pltpu.VMEM((views * det, channels), bf),
                pltpu.VMEM((views * det, channels), f32),
                pltpu.VMEM((10, rows, plane), bf),
                pltpu.VMEM((2, 1, plane), f32),
                pltpu.VMEM((2, 1, plane), f32),
                pltpu.VMEM((total_rows, views * det), bf),
                pltpu.VMEM((views * det, total_rows), bf),
                pltpu.VMEM((total_rows, channels), bf),
                pltpu.VMEM((total_rows, channels), bf),
                pltpu.VMEM((views * det, channels), f32),
                pltpu.VMEM((views * det, channels), bf),
                pltpu.VMEM((total_rows, channels), bf),
                pltpu.VMEM((10, rows, plane), f32),
                pltpu.VMEM((rows, plane), bf),
                pltpu.VMEM((5, rows, plane), f32),
                pltpu.VMEM((4, rows, plane), bf),
                pltpu.VMEM((4, rows, plane), bf),
                dma((7,)),
                dma((4,)),
                dma((4,)),
                dma((5,)),
                dma((5,)),
                dma((2,)),
                dma((2,)),
                dma((5,)),
                dma((5,)),
                dma((4,)),
                dma((4,)),
                dma((1,)),
                dma((1,)),
                dma((2,)),
                pltpu.SemaphoreType.REGULAR((2,)),
            ],
            compiler_params=pltpu.CompilerParams(
                collective_id=0, has_side_effects=True, vmem_limit_bytes=67_043_328
            ),
            name="ct_gradient",
        )(
            angle_index,
            cover.T,
            offset.T,
            count,
            volume.reshape(rows, strip, width // 128, 128).transpose(0, 2, 1, 3).reshape(-1, 128),
            footprint.reshape(tables, plane, channels),
            measured.reshape(views * det, channels),
        )
        return gradient.reshape(rows, width // 128, strip, 128).transpose(0, 2, 1, 3).reshape(volume.shape)

    axes = ("grp", "view")
    in_specs = (
        P(axes, None, None, None),
        P(axes, None, None, None),
        P(axes, None, None),
        P(axes),
        P(axes, None),
        P(axes, None),
        P(axes),
    )
    return jax.shard_map(
        shards, mesh=mesh, in_specs=in_specs, out_specs=P(axes, None, None, None), check_vma=False
    )
```

```python
import jax
import jax.numpy as jnp
from jax import lax
from jax.experimental import pallas as pl
from jax.experimental.pallas import tpu as pltpu
from jax.sharding import PartitionSpec as P

DELTA = 0.5
PRIOR_WEIGHT = 2.0
MESH = pl.DeviceIdType.MESH
HOPS = (1, -1, 2, -2)
BACK = (1, 0, 3, 2)
GRAD_SLOT = (0, 4, 2, 6, 8)
CORES = 2
LINE = 8
NT = (((1,), (1,)), ((), ()))


def chunks(total, width):
    return [(at, min(width, total - at)) for at in range(0, total, width)]


def kernel(
    n_grp,
    n_view,
    angle_hbm,
    cover_hbm,
    offset_hbm,
    count_hbm,
    vol_hbm,
    fp_hbm,
    meas_hbm,
    out_hbm,
    prior_hbm,
    angle_ref,
    cover_ref,
    offset_ref,
    count_ref,
    raw,
    vol_ref,
    fp,
    meas,
    gain,
    win,
    edge,
    halo,
    sel,
    sel_t,
    hi,
    lo,
    proj,
    wres,
    gsum,
    gwin,
    box,
    from_partner,
    out_bf,
    arrived,
    load_sem,
    vol_send,
    vol_recv,
    pass_send,
    pass_recv,
    edge_send,
    edge_recv,
    pg_send,
    pg_recv,
    og_send,
    og_recv,
    box_send,
    box_recv,
    fwd_send,
    here_sem,
    out_ref,
    prior_ref,
    store_sem,
):
    n_dev = n_grp * n_view
    n_chip = n_dev // CORES
    me = lax.axis_index("grp") * n_view + lax.axis_index("view")
    chip = me // CORES
    core = me % CORES
    tables, plane, channels = fp.shape
    views = angle_ref.shape[0]
    slots = cover_ref.shape[0]
    rows = vol_ref.shape[0]
    slab = rows // 2
    pieces = plane // 128
    det = meas.shape[0] // views
    chip_rows = CORES * rows
    first_rows, last_rows = 3 * chip_rows, 2 * chip_rows
    first_all = tables * first_rows
    side_all = tables * last_rows
    total_rows = tables * 5 * chip_rows
    in_line = chip % LINE
    line = chip // LINE
    span = CORES * LINE
    line_below, line_above = line > 0, line < n_chip // LINE - 1

    def at(device):
        return (device // n_view, device % n_view)

    def exists(hop):
        return jnp.logical_and(chip + hop >= 0, chip + hop < n_chip)

    def peer(hop):
        return at(jnp.clip(me + CORES * hop, 0, n_dev - 1))

    partner = at(me + 1 - 2 * core)
    below, above = me - 1, me + 1
    has_below, has_above = below >= 0, above < n_dev

    def crosses(hop):
        return jnp.logical_or(in_line + hop < 0, in_line + hop >= LINE)

    def direct(hop):
        return jnp.logical_and(exists(hop), jnp.logical_not(crosses(hop))) if hop < 0 else exists(hop)

    relay = jnp.logical_and(in_line < 2, line_above)
    boxed = jnp.logical_and(in_line < 2, line_below)
    tail = jnp.logical_and(in_line == LINE - 1, line_above)
    to_tail = span - CORES * (1 + in_line)

    def device_at(offset):
        return at(jnp.clip(me + offset, 0, n_dev - 1))

    barrier = pltpu.get_barrier_semaphore()
    expected = jnp.int32(1)

    def greet(allowed, offset, count=1):
        @pl.when(allowed)
        def _():
            pl.semaphore_signal(barrier, inc=count, device_id=device_at(offset), device_id_type=MESH)

    for hop in HOPS:
        if hop > 0:
            greet(jnp.logical_and(exists(hop), jnp.logical_not(crosses(hop))), CORES * hop)
        else:
            greet(exists(hop), CORES * hop)
        expected = expected + direct(hop).astype(jnp.int32)
    greet(relay, span)
    greet(relay, to_tail)
    expected = expected + boxed.astype(jnp.int32) + 2 * tail.astype(jnp.int32)
    pl.semaphore_signal(barrier, inc=1, device_id=partner, device_id_type=MESH)
    greet(jnp.logical_and(core == 0, has_below), -1)
    greet(jnp.logical_and(core == 1, jnp.logical_and(has_above, in_line < LINE - 1)), 1)
    expected = expected + jnp.logical_and(core == 1, has_above).astype(jnp.int32)
    expected = expected + jnp.logical_and(core == 0, in_line > 0).astype(jnp.int32)

    loads = [
        pltpu.make_async_copy(source, target, load_sem.at[n])
        for n, (source, target) in enumerate(
            (
                (vol_hbm, raw),
                (angle_hbm, angle_ref),
                (cover_hbm, cover_ref),
                (offset_hbm, offset_ref),
                (count_hbm, count_ref),
                (meas_hbm, meas),
                (fp_hbm, fp),
            )
        )
    ]
    for copy in loads:
        copy.start()
    pl.semaphore_wait(barrier, expected)

    for offset in (CORES - span, 2 * CORES - span):

        @pl.when(tail)
        def _(offset=offset):
            pl.semaphore_signal(here_sem.at[0], inc=1, device_id=device_at(offset), device_id_type=MESH)

    loads[0].wait()
    for piece in range(pieces):
        at_column = ((piece % 2) * (pieces // 2) + piece // 2) * 128
        value = raw[pl.ds(piece, rows, stride=pieces), :]
        vol_ref[:, pl.ds(at_column, 128)] = value
        win[core, :, pl.ds(at_column, 128)] = value.astype(jnp.bfloat16)
    edge[0] = vol_ref[0:1, :]
    edge[1] = vol_ref[rows - 1 : rows, :]

    for j, hop in enumerate(HOPS):

        @pl.when(jnp.logical_not(exists(hop)))
        def _(j=j):
            win[2 + 2 * j] = jnp.zeros_like(win[2 + 2 * j])
            win[3 + 2 * j] = jnp.zeros_like(win[3 + 2 * j])
            arrived[j] = jnp.zeros_like(arrived[j])

    @pl.when(jnp.logical_not(has_below))
    def _():
        halo[0] = jnp.zeros_like(halo[0])

    @pl.when(jnp.logical_not(has_above))
    def _():
        halo[1] = jnp.zeros_like(halo[1])


    vol_copies = [
        pltpu.make_async_remote_copy(
            src_ref=win.at[core],
            dst_ref=win.at[2 + 2 * BACK[j] + core],
            send_sem=vol_send.at[j],
            recv_sem=vol_recv.at[BACK[j]],
            device_id=peer(hop),
            device_id_type=MESH,
        )
        for j, hop in enumerate(HOPS)
    ]
    box_copy = pltpu.make_async_remote_copy(
        src_ref=win.at[core],
        dst_ref=box,
        send_sem=box_send.at[0],
        recv_sem=box_recv.at[0],
        device_id=device_at(-span),
        device_id_type=MESH,
    )
    fwd_copy = pltpu.make_async_remote_copy(
        src_ref=box,
        dst_ref=win.at[2 + 4 * in_line + core],
        send_sem=fwd_send.at[0],
        recv_sem=vol_recv.at[2 * in_line],
        device_id=device_at(to_tail),
        device_id_type=MESH,
    )
    step_copy = pltpu.make_async_remote_copy(
        src_ref=win.at[2 + core],
        dst_ref=win.at[6 + core],
        send_sem=fwd_send.at[1],
        recv_sem=vol_recv.at[2],
        device_id=device_at(-CORES),
        device_id_type=MESH,
    )
    window_slot = [2 + 2 * j for j in range(4)] + [0]
    pass_copies = [
        pltpu.make_async_remote_copy(
            src_ref=win.at[slot + core],
            dst_ref=win.at[slot + core],
            send_sem=pass_send.at[j],
            recv_sem=pass_recv.at[j],
            device_id=partner,
            device_id_type=MESH,
        )
        for j, slot in enumerate(window_slot)
    ]
    edge_copies = [
        pltpu.make_async_remote_copy(
            src_ref=edge.at[side],
            dst_ref=halo.at[1 - side],
            send_sem=edge_send.at[side],
            recv_sem=edge_recv.at[1 - side],
            device_id=device_at(2 * side - 1),
            device_id_type=MESH,
        )
        for side in range(2)
    ]

    @pl.when(boxed)
    def _():
        box_copy.start()

    for j in range(4):

        @pl.when(direct(HOPS[j]))
        def _(j=j):
            vol_copies[j].start()

    pass_copies[4].start()
    edge_waits = jnp.logical_and(core == 0, in_line == 0)

    @pl.when(jnp.logical_and(has_below, jnp.logical_not(edge_waits)))
    def _():
        edge_copies[0].start()

    @pl.when(has_above)
    def _():
        edge_copies[1].start()

    for copy in loads[1:5]:
        copy.wait()

    first_block = (chip - 2) * 4
    row_of = []
    for v in range(views):
        here = []
        for k in range(slots):
            block = cover_ref[k, v] - first_block
            distance = block // 4 - 2
            reach = jnp.abs(distance)
            within = (block % 4) * slab
            table = angle_ref[v]
            off = offset_ref[k, v]
            under = jnp.where(distance < 0, 1, 0)
            place = jnp.where(reach == 0, 0, 2 * reach - 1 + under) * chip_rows + within
            ahead = jnp.where(
                reach < 2, table * first_rows + place, first_all + table * last_rows + place - first_rows
            )
            side = under * side_all + table * last_rows + (reach - 1) * chip_rows + within
            behind = jnp.where(reach > 0, side, 2 * side_all + table * chip_rows + within)
            here.append((ahead - off, behind - off, off, k < count_ref[v]))
        row_of.append(here)

    det_iota = lax.broadcasted_iota(jnp.int32, (det, 128), 0)
    for v in range(views):
        goals = []
        for row, _, off, live in row_of[v]:
            off_live = jnp.where(live, off, -4096)
            inside = jnp.logical_and(det_iota >= off_live, det_iota < off_live + slab)
            goals.append(jnp.where(inside, det_iota + row, -1))
        for tile in range(total_rows // 128):
            lane = lax.broadcasted_iota(jnp.int32, (det, 128), 1) + tile * 128
            hits = jnp.zeros((det, 128), jnp.float32)
            for goal in goals:
                hits = hits + jnp.where(goal == lane, 1.0, 0.0)
            sel_t[pl.ds(v * det, det), pl.ds(tile * 128, 128)] = hits.astype(jnp.bfloat16)
    lane = lax.broadcasted_iota(jnp.int32, (8, views * det), 1)
    goals = []
    for k in range(slots):
        goal = jnp.full((8, views * det), -1, jnp.int32)
        for v in range(views):
            _, row, off, live = row_of[v][k]
            off_live = jnp.where(live, off, -4096)
            spot = lane - v * det
            inside = jnp.logical_and(
                jnp.logical_and(spot >= off_live, spot < off_live + slab),
                jnp.logical_and(spot >= 0, spot < det),
            )
            goal = jnp.where(inside, spot + row, goal)
        goals.append(goal[0:1, :])

    def build_sel(step, _):
        at_row = pl.multiple_of(step * 32, 32)
        index = lax.broadcasted_iota(jnp.int32, (32, views * det), 0) + step * 32
        hits = jnp.zeros((32, views * det), jnp.float32)
        for goal in goals:
            hits = hits + jnp.where(goal == index, 1.0, 0.0)
        sel[pl.ds(at_row, 32), :] = hits.astype(jnp.bfloat16)
        return 0

    lax.fori_loop(0, total_rows // 32, build_sel, 0)

    loads[5].wait()

    def build_gain(step, _):
        part = pl.ds(pl.multiple_of(step * 32, 32), 32)
        gain[part, :] = jnp.exp(-meas[part, :].astype(jnp.float32))
        return 0

    lax.fori_loop(0, meas.shape[0] // 32, build_gain, 0)
    loads[6].wait()

    def project(first_slot, slot_count, first_row):
        block = win[pl.ds(first_slot, slot_count)].reshape(slot_count * rows, plane)
        height = slot_count * rows
        for table in range(tables):
            for start, width in chunks(channels, 256):
                cols = pl.ds(start, width)
                product = jnp.dot(block, fp[table, :, cols], preferred_element_type=jnp.float32)
                top = product.astype(jnp.bfloat16)
                part = pl.ds(first_row + table * height, height)
                hi[part, cols] = top
                lo[part, cols] = (product - top.astype(jnp.float32)).astype(jnp.bfloat16)

    def placed(first_row, height, cols):
        pick = sel_t[:, pl.ds(first_row, height)]
        part = pl.ds(first_row, height)
        return jnp.dot(pick, hi[part, cols], preferred_element_type=jnp.float32) + jnp.dot(
            pick, lo[part, cols], preferred_element_type=jnp.float32
        )

    def collect(which):
        for j in which:

            @pl.when(exists(HOPS[j]))
            def _(j=j):
                vol_copies[BACK[j]].wait_recv()
                pass_copies[j].start()

            if j == 0:

                @pl.when(tail)
                def _():
                    step_copy.start()

        for j in which:

            @pl.when(exists(HOPS[j]))
            def _(j=j):
                pass_copies[j].wait_recv()

    @pl.when(relay)
    def _():
        box_copy.wait_recv()
        pl.semaphore_wait(here_sem.at[0], 1)
        fwd_copy.start()

    pass_copies[4].wait_recv()
    collect((0, 1))

    @pl.when(jnp.logical_and(has_below, edge_waits))
    def _():
        edge_copies[0].start()

    project(0, 6, 0)
    for start, width in chunks(channels, 256):
        cols = pl.ds(start, width)
        proj[:, cols] = placed(0, first_all, cols)
    collect((2, 3))
    project(6, 4, first_all)
    for start, width in chunks(channels, 256):
        cols = pl.ds(start, width)
        forward = proj[:, cols] + placed(first_all, side_all, cols)
        wres[:, cols] = (gain[:, cols] * (forward - meas[:, cols].astype(jnp.float32))).astype(jnp.bfloat16)

    def gather(first_row, height):
        part = pl.ds(first_row, height)
        for start, width in chunks(channels, 256):
            cols = pl.ds(start, width)
            gsum[part, cols] = jnp.dot(sel[part, :], wres[:, cols], preferred_element_type=jnp.float32).astype(
                jnp.bfloat16
            )

    def backproject(first_row, stride, first_slot, slot_count):
        height = slot_count * rows
        for start, width in chunks(plane, 256):
            total = None
            for table in range(tables):
                term = lax.dot_general(
                    gsum[pl.ds(first_row + table * stride, height), :],
                    fp[table, pl.ds(start, width), :],
                    NT,
                    preferred_element_type=jnp.float32,
                )
                total = term if total is None else total + term
            gwin[pl.ds(first_slot, slot_count), :, pl.ds(start, width)] = total.reshape(slot_count, rows, width)

    pg_copies = [
        pltpu.make_async_remote_copy(
            src_ref=gwin.at[GRAD_SLOT[j] + 1 - core],
            dst_ref=from_partner.at[j],
            send_sem=pg_send.at[j],
            recv_sem=pg_recv.at[j],
            device_id=partner,
            device_id_type=MESH,
        )
        for j in range(5)
    ]
    og_copies = [
        pltpu.make_async_remote_copy(
            src_ref=out_bf.at[j],
            dst_ref=arrived.at[BACK[j]],
            send_sem=og_send.at[j],
            recv_sem=og_recv.at[BACK[j]],
            device_id=peer(hop),
            device_id_type=MESH,
        )
        for j, hop in enumerate(HOPS)
    ]

    def hand_out(which):
        for j in which:
            pg_copies[j].wait_recv()
            out_bf[j] = (gwin[GRAD_SLOT[j] + core] + from_partner[j]).astype(jnp.bfloat16)

            @pl.when(exists(HOPS[j]))
            def _(j=j):
                og_copies[j].start()

    gather(0, side_all)
    backproject(0, last_rows, 0, 4)
    pg_copies[0].start()
    pg_copies[2].start()
    gather(side_all, side_all)
    hand_out((0, 2))
    backproject(side_all, last_rows, 4, 4)
    pg_copies[1].start()
    pg_copies[3].start()
    gather(2 * side_all, tables * chip_rows)
    hand_out((1, 3))
    backproject(2 * side_all, chip_rows, 8, 2)
    pg_copies[4].start()

    @pl.when(has_below)
    def _():
        edge_copies[1].wait_recv()

    @pl.when(has_above)
    def _():
        edge_copies[0].wait_recv()

    here = vol_ref[...]
    row = lax.broadcasted_iota(jnp.int32, here.shape, 0)
    column = lax.broadcasted_iota(jnp.int32, here.shape, 1) % (plane // 2)

    def step_to(other, allowed):
        return jnp.where(allowed, jnp.clip(here - other, -DELTA, DELTA), 0.0)

    lower = jnp.where(row == 0, halo[0], pltpu.roll(here, 1, 0))
    upper = jnp.where(row == rows - 1, halo[1], pltpu.roll(here, rows - 1, 0))
    prior = step_to(lower, row + me > 0)
    prior = prior + step_to(upper, row + (me + 1 - n_dev) < rows - 1)
    prior = prior + jnp.clip(here - pltpu.roll(here, plane // 2, 1), -DELTA, DELTA)
    prior = prior + step_to(pltpu.roll(here, 1, 1), column > 0)
    prior = prior + step_to(pltpu.roll(here, plane - 1, 1), column < plane // 2 - 1)
    prior = PRIOR_WEIGHT * prior
    for piece in range(pieces):
        at_column = ((piece % 2) * (pieces // 2) + piece // 2) * 128
        prior_ref[pl.ds(piece, rows, stride=pieces), :] = prior[:, at_column : at_column + 128]
    prior_store = pltpu.make_async_copy(prior_ref, prior_hbm, store_sem.at[0])
    prior_store.start()

    pg_copies[4].wait_recv()
    total = gwin[8 + core] + from_partner[4]
    for j in range(4):

        @pl.when(exists(HOPS[j]))
        def _(j=j):
            og_copies[BACK[j]].wait_recv()

        total = total + arrived[j].astype(jnp.float32)
    for piece in range(pieces):
        at_column = ((piece % 2) * (pieces // 2) + piece // 2) * 128
        out_ref[pl.ds(piece, rows, stride=pieces), :] = total[:, at_column : at_column + 128]
    out_store = pltpu.make_async_copy(out_ref, out_hbm, store_sem.at[1])
    out_store.start()

    for j, hop in enumerate(HOPS):

        @pl.when(direct(hop))
        def _(j=j):
            vol_copies[j].wait_send()

        @pl.when(exists(hop))
        def _(j=j):
            pass_copies[j].wait_send()
            og_copies[j].wait_send()

    @pl.when(boxed)
    def _():
        box_copy.wait_send()

    @pl.when(relay)
    def _():
        fwd_copy.wait_send()

    @pl.when(tail)
    def _():
        step_copy.wait_send()

    pass_copies[4].wait_send()
    for j in range(5):
        pg_copies[j].wait_send()

    @pl.when(has_below)
    def _():
        edge_copies[0].wait_send()

    @pl.when(has_above)
    def _():
        edge_copies[1].wait_send()

    prior_store.wait()
    out_store.wait()


def solution(mesh):
    n_grp, n_view = mesh.shape["grp"], mesh.shape["view"]

    def shards(volume, footprint, measured, angle_index, cover, offset, count):
        blocks, slab, strip, width = volume.shape
        views, det, channels = measured.shape
        tables = footprint.shape[0]
        rows, plane = blocks * slab, strip * width
        total_rows = tables * 5 * CORES * rows
        bf, f32 = jnp.bfloat16, jnp.float32
        dma = pltpu.SemaphoreType.DMA
        hbm = pl.BlockSpec(memory_space=pltpu.HBM)
        data, prior = pl.pallas_call(
            lambda *refs: kernel(n_grp, n_view, *refs),
            out_shape=[jax.ShapeDtypeStruct((rows * plane // 128, 128), f32)] * 2,
            in_specs=[hbm] * 7,
            out_specs=[hbm, hbm],
            scratch_shapes=[
                pltpu.SMEM(angle_index.shape, jnp.int32),
                pltpu.SMEM(cover.T.shape, jnp.int32),
                pltpu.SMEM(offset.T.shape, jnp.int32),
                pltpu.SMEM(count.shape, jnp.int32),
                pltpu.VMEM((rows * plane // 128, 128), f32),
                pltpu.VMEM((rows, plane), f32),
                pltpu.VMEM((tables, plane, channels), bf),
                pltpu.VMEM((views * det, channels), bf),
                pltpu.VMEM((views * det, channels), f32),
                pltpu.VMEM((10, rows, plane), bf),
                pltpu.VMEM((2, 1, plane), f32),
                pltpu.VMEM((2, 1, plane), f32),
                pltpu.VMEM((total_rows, views * det), bf),
                pltpu.VMEM((views * det, total_rows), bf),
                pltpu.VMEM((total_rows, channels), bf),
                pltpu.VMEM((total_rows, channels), bf),
                pltpu.VMEM((views * det, channels), f32),
                pltpu.VMEM((views * det, channels), bf),
                pltpu.VMEM((total_rows, channels), bf),
                pltpu.VMEM((10, rows, plane), f32),
                pltpu.VMEM((rows, plane), bf),
                pltpu.VMEM((5, rows, plane), f32),
                pltpu.VMEM((4, rows, plane), bf),
                pltpu.VMEM((4, rows, plane), bf),
                dma((7,)),
                dma((4,)),
                dma((4,)),
                dma((5,)),
                dma((5,)),
                dma((2,)),
                dma((2,)),
                dma((5,)),
                dma((5,)),
                dma((4,)),
                dma((4,)),
                dma((1,)),
                dma((1,)),
                dma((2,)),
                pltpu.SemaphoreType.REGULAR((1,)),
                pltpu.VMEM((rows * plane // 128, 128), f32),
                pltpu.VMEM((rows * plane // 128, 128), f32),
                dma((2,)),
            ],
            compiler_params=pltpu.CompilerParams(
                collective_id=0, has_side_effects=True, vmem_limit_bytes=67_043_328
            ),
            name="ct_gradient",
        )(
            angle_index,
            cover.T,
            offset.T,
            count,
            volume.reshape(rows, strip, width // 128, 128).transpose(0, 2, 1, 3).reshape(-1, 128),
            footprint.reshape(tables, plane, channels),
            measured.reshape(views * det, channels),
        )
        gradient = data + prior
        return gradient.reshape(rows, width // 128, strip, 128).transpose(0, 2, 1, 3).reshape(volume.shape)

    axes = ("grp", "view")
    in_specs = (
        P(axes, None, None, None),
        P(axes, None, None, None),
        P(axes, None, None),
        P(axes),
        P(axes, None),
        P(axes, None),
        P(axes),
    )
    return jax.shard_map(
        shards, mesh=mesh, in_specs=in_specs, out_specs=P(axes, None, None, None), check_vma=False
    )
```

```python
import jax
import jax.numpy as jnp
from jax import lax
from jax.experimental import pallas as pl
from jax.experimental.pallas import tpu as pltpu
from jax.sharding import PartitionSpec as P

DELTA = 0.5
PRIOR_WEIGHT = 2.0
MESH = pl.DeviceIdType.MESH
HOPS = (1, -1, 2, -2)
BACK = (1, 0, 3, 2)
GRAD_SLOT = (0, 4, 2, 6, 8)
CORES = 2
LINE = 8
NT = (((1,), (1,)), ((), ()))


def chunks(total, width):
    return [(at, min(width, total - at)) for at in range(0, total, width)]


def kernel(
    n_grp,
    n_view,
    angle_hbm,
    cover_hbm,
    offset_hbm,
    count_hbm,
    vol_hbm,
    fp_hbm,
    meas_hbm,
    out_ref,
    prior_ref,
    angle_ref,
    cover_ref,
    offset_ref,
    count_ref,
    raw,
    vol_ref,
    fp,
    meas,
    gain,
    win,
    edge,
    halo,
    sel,
    sel_t,
    hi,
    lo,
    proj,
    wres,
    gsum,
    gwin,
    box,
    from_partner,
    out_bf,
    arrived,
    load_sem,
    vol_send,
    vol_recv,
    pass_send,
    pass_recv,
    edge_send,
    edge_recv,
    pg_send,
    pg_recv,
    og_send,
    og_recv,
    box_send,
    box_recv,
    fwd_send,
    here_sem,
):
    n_dev = n_grp * n_view
    n_chip = n_dev // CORES
    me = lax.axis_index("grp") * n_view + lax.axis_index("view")
    chip = me // CORES
    core = me % CORES
    tables, plane, channels = fp.shape
    views = angle_ref.shape[0]
    slots = cover_ref.shape[0]
    rows = vol_ref.shape[0]
    slab = rows // 2
    pieces = plane // 128
    det = meas.shape[0] // views
    chip_rows = CORES * rows
    first_rows, last_rows = 3 * chip_rows, 2 * chip_rows
    first_all = tables * first_rows
    side_all = tables * last_rows
    total_rows = tables * 5 * chip_rows
    in_line = chip % LINE
    line = chip // LINE
    span = CORES * LINE
    line_below, line_above = line > 0, line < n_chip // LINE - 1

    def at(device):
        return (device // n_view, device % n_view)

    def exists(hop):
        return jnp.logical_and(chip + hop >= 0, chip + hop < n_chip)

    def peer(hop):
        return at(jnp.clip(me + CORES * hop, 0, n_dev - 1))

    partner = at(me + 1 - 2 * core)
    below, above = me - 1, me + 1
    has_below, has_above = below >= 0, above < n_dev

    def crosses(hop):
        return jnp.logical_or(in_line + hop < 0, in_line + hop >= LINE)

    def direct(hop):
        return jnp.logical_and(exists(hop), jnp.logical_not(crosses(hop))) if hop < 0 else exists(hop)

    relay = jnp.logical_and(in_line < 2, line_above)
    boxed = jnp.logical_and(in_line < 2, line_below)
    tail = jnp.logical_and(in_line == LINE - 1, line_above)
    to_tail = span - CORES * (1 + in_line)

    def device_at(offset):
        return at(jnp.clip(me + offset, 0, n_dev - 1))

    barrier = pltpu.get_barrier_semaphore()
    expected = jnp.int32(1)

    def greet(allowed, offset, count=1):
        @pl.when(allowed)
        def _():
            pl.semaphore_signal(barrier, inc=count, device_id=device_at(offset), device_id_type=MESH)

    for hop in HOPS:
        if hop > 0:
            greet(jnp.logical_and(exists(hop), jnp.logical_not(crosses(hop))), CORES * hop)
        else:
            greet(exists(hop), CORES * hop)
        expected = expected + direct(hop).astype(jnp.int32)
    greet(relay, span)
    greet(relay, to_tail)
    expected = expected + boxed.astype(jnp.int32) + 2 * tail.astype(jnp.int32)
    pl.semaphore_signal(barrier, inc=1, device_id=partner, device_id_type=MESH)
    greet(jnp.logical_and(core == 0, has_below), -1)
    greet(jnp.logical_and(core == 1, jnp.logical_and(has_above, in_line < LINE - 1)), 1)
    expected = expected + jnp.logical_and(core == 1, has_above).astype(jnp.int32)
    expected = expected + jnp.logical_and(core == 0, in_line > 0).astype(jnp.int32)

    loads = [
        pltpu.make_async_copy(source, target, load_sem.at[n])
        for n, (source, target) in enumerate(
            (
                (vol_hbm, raw),
                (angle_hbm, angle_ref),
                (cover_hbm, cover_ref),
                (offset_hbm, offset_ref),
                (count_hbm, count_ref),
                (meas_hbm, meas),
                (fp_hbm, fp),
            )
        )
    ]
    for copy in loads:
        copy.start()
    pl.semaphore_wait(barrier, expected)

    for offset in (CORES - span, 2 * CORES - span):

        @pl.when(tail)
        def _(offset=offset):
            pl.semaphore_signal(here_sem.at[0], inc=1, device_id=device_at(offset), device_id_type=MESH)

    loads[0].wait()
    for piece in range(pieces):
        at_column = ((piece % 2) * (pieces // 2) + piece // 2) * 128
        value = raw[pl.ds(piece, rows, stride=pieces), :]
        vol_ref[:, pl.ds(at_column, 128)] = value
        win[core, :, pl.ds(at_column, 128)] = value.astype(jnp.bfloat16)
    edge[0] = vol_ref[0:1, :]
    edge[1] = vol_ref[rows - 1 : rows, :]

    for j, hop in enumerate(HOPS):

        @pl.when(jnp.logical_not(exists(hop)))
        def _(j=j):
            win[2 + 2 * j] = jnp.zeros_like(win[2 + 2 * j])
            win[3 + 2 * j] = jnp.zeros_like(win[3 + 2 * j])
            arrived[j] = jnp.zeros_like(arrived[j])

    @pl.when(jnp.logical_not(has_below))
    def _():
        halo[0] = jnp.zeros_like(halo[0])

    @pl.when(jnp.logical_not(has_above))
    def _():
        halo[1] = jnp.zeros_like(halo[1])


    vol_copies = [
        pltpu.make_async_remote_copy(
            src_ref=win.at[core],
            dst_ref=win.at[2 + 2 * BACK[j] + core],
            send_sem=vol_send.at[j],
            recv_sem=vol_recv.at[BACK[j]],
            device_id=peer(hop),
            device_id_type=MESH,
        )
        for j, hop in enumerate(HOPS)
    ]
    box_copy = pltpu.make_async_remote_copy(
        src_ref=win.at[core],
        dst_ref=box,
        send_sem=box_send.at[0],
        recv_sem=box_recv.at[0],
        device_id=device_at(-span),
        device_id_type=MESH,
    )
    fwd_copy = pltpu.make_async_remote_copy(
        src_ref=box,
        dst_ref=win.at[2 + 4 * in_line + core],
        send_sem=fwd_send.at[0],
        recv_sem=vol_recv.at[2 * in_line],
        device_id=device_at(to_tail),
        device_id_type=MESH,
    )
    step_copy = pltpu.make_async_remote_copy(
        src_ref=win.at[2 + core],
        dst_ref=win.at[6 + core],
        send_sem=fwd_send.at[1],
        recv_sem=vol_recv.at[2],
        device_id=device_at(-CORES),
        device_id_type=MESH,
    )
    window_slot = [2 + 2 * j for j in range(4)] + [0]
    pass_copies = [
        pltpu.make_async_remote_copy(
            src_ref=win.at[slot + core],
            dst_ref=win.at[slot + core],
            send_sem=pass_send.at[j],
            recv_sem=pass_recv.at[j],
            device_id=partner,
            device_id_type=MESH,
        )
        for j, slot in enumerate(window_slot)
    ]
    edge_copies = [
        pltpu.make_async_remote_copy(
            src_ref=edge.at[side],
            dst_ref=halo.at[1 - side],
            send_sem=edge_send.at[side],
            recv_sem=edge_recv.at[1 - side],
            device_id=device_at(2 * side - 1),
            device_id_type=MESH,
        )
        for side in range(2)
    ]

    @pl.when(boxed)
    def _():
        box_copy.start()

    for j in range(4):

        @pl.when(direct(HOPS[j]))
        def _(j=j):
            vol_copies[j].start()

    pass_copies[4].start()
    edge_waits = jnp.logical_and(core == 0, in_line == 0)

    @pl.when(jnp.logical_and(has_below, jnp.logical_not(edge_waits)))
    def _():
        edge_copies[0].start()

    @pl.when(has_above)
    def _():
        edge_copies[1].start()

    for copy in loads[1:5]:
        copy.wait()

    first_block = (chip - 2) * 4
    row_of = []
    for v in range(views):
        here = []
        for k in range(slots):
            block = cover_ref[k, v] - first_block
            distance = block // 4 - 2
            reach = jnp.abs(distance)
            within = (block % 4) * slab
            table = angle_ref[v]
            off = offset_ref[k, v]
            under = jnp.where(distance < 0, 1, 0)
            place = jnp.where(reach == 0, 0, 2 * reach - 1 + under) * chip_rows + within
            ahead = jnp.where(
                reach < 2, table * first_rows + place, first_all + table * last_rows + place - first_rows
            )
            side = under * side_all + table * last_rows + (reach - 1) * chip_rows + within
            behind = jnp.where(reach > 0, side, 2 * side_all + table * chip_rows + within)
            here.append((ahead - off, behind - off, off, k < count_ref[v]))
        row_of.append(here)

    det_iota = lax.broadcasted_iota(jnp.int32, (det, 128), 0)
    for v in range(views):
        goals = []
        for row, _, off, live in row_of[v]:
            off_live = jnp.where(live, off, -4096)
            inside = jnp.logical_and(det_iota >= off_live, det_iota < off_live + slab)
            goals.append(jnp.where(inside, det_iota + row, -1))
        for tile in range(total_rows // 128):
            lane = lax.broadcasted_iota(jnp.int32, (det, 128), 1) + tile * 128
            hits = jnp.zeros((det, 128), jnp.float32)
            for goal in goals:
                hits = hits + jnp.where(goal == lane, 1.0, 0.0)
            sel_t[pl.ds(v * det, det), pl.ds(tile * 128, 128)] = hits.astype(jnp.bfloat16)
    lane = lax.broadcasted_iota(jnp.int32, (8, views * det), 1)
    goals = []
    for k in range(slots):
        goal = jnp.full((8, views * det), -1, jnp.int32)
        for v in range(views):
            _, row, off, live = row_of[v][k]
            off_live = jnp.where(live, off, -4096)
            spot = lane - v * det
            inside = jnp.logical_and(
                jnp.logical_and(spot >= off_live, spot < off_live + slab),
                jnp.logical_and(spot >= 0, spot < det),
            )
            goal = jnp.where(inside, spot + row, goal)
        goals.append(goal[0:1, :])

    def build_sel(step, _):
        at_row = pl.multiple_of(step * 32, 32)
        index = lax.broadcasted_iota(jnp.int32, (32, views * det), 0) + step * 32
        hits = jnp.zeros((32, views * det), jnp.float32)
        for goal in goals:
            hits = hits + jnp.where(goal == index, 1.0, 0.0)
        sel[pl.ds(at_row, 32), :] = hits.astype(jnp.bfloat16)
        return 0

    lax.fori_loop(0, total_rows // 32, build_sel, 0)

    loads[5].wait()

    def build_gain(step, _):
        part = pl.ds(pl.multiple_of(step * 32, 32), 32)
        gain[part, :] = jnp.exp(-meas[part, :].astype(jnp.float32))
        return 0

    lax.fori_loop(0, meas.shape[0] // 32, build_gain, 0)
    loads[6].wait()

    def project(first_slot, slot_count, first_row):
        block = win[pl.ds(first_slot, slot_count)].reshape(slot_count * rows, plane)
        height = slot_count * rows
        for table in range(tables):
            for start, width in chunks(channels, 256):
                cols = pl.ds(start, width)
                product = jnp.dot(block, fp[table, :, cols], preferred_element_type=jnp.float32)
                top = product.astype(jnp.bfloat16)
                part = pl.ds(first_row + table * height, height)
                hi[part, cols] = top
                lo[part, cols] = (product - top.astype(jnp.float32)).astype(jnp.bfloat16)

    def placed(first_row, height, cols):
        pick = sel_t[:, pl.ds(first_row, height)]
        part = pl.ds(first_row, height)
        return jnp.dot(pick, hi[part, cols], preferred_element_type=jnp.float32) + jnp.dot(
            pick, lo[part, cols], preferred_element_type=jnp.float32
        )

    def collect(which):
        for j in which:

            @pl.when(exists(HOPS[j]))
            def _(j=j):
                vol_copies[BACK[j]].wait_recv()
                pass_copies[j].start()

            if j == 0:

                @pl.when(tail)
                def _():
                    step_copy.start()

        for j in which:

            @pl.when(exists(HOPS[j]))
            def _(j=j):
                pass_copies[j].wait_recv()

    @pl.when(relay)
    def _():
        box_copy.wait_recv()
        pl.semaphore_wait(here_sem.at[0], 1)
        fwd_copy.start()

    pass_copies[4].wait_recv()
    collect((0, 1))

    @pl.when(jnp.logical_and(has_below, edge_waits))
    def _():
        edge_copies[0].start()

    project(0, 6, 0)
    for start, width in chunks(channels, 256):
        cols = pl.ds(start, width)
        proj[:, cols] = placed(0, first_all, cols)
    collect((2, 3))
    project(6, 4, first_all)
    for start, width in chunks(channels, 256):
        cols = pl.ds(start, width)
        forward = proj[:, cols] + placed(first_all, side_all, cols)
        wres[:, cols] = (gain[:, cols] * (forward - meas[:, cols].astype(jnp.float32))).astype(jnp.bfloat16)

    def gather(first_row, height):
        part = pl.ds(first_row, height)
        for start, width in chunks(channels, 256):
            cols = pl.ds(start, width)
            gsum[part, cols] = jnp.dot(sel[part, :], wres[:, cols], preferred_element_type=jnp.float32).astype(
                jnp.bfloat16
            )

    def backproject(first_row, stride, first_slot, slot_count):
        height = slot_count * rows
        for start, width in chunks(plane, 256):
            total = None
            for table in range(tables):
                term = lax.dot_general(
                    gsum[pl.ds(first_row + table * stride, height), :],
                    fp[table, pl.ds(start, width), :],
                    NT,
                    preferred_element_type=jnp.float32,
                )
                total = term if total is None else total + term
            gwin[pl.ds(first_slot, slot_count), :, pl.ds(start, width)] = total.reshape(slot_count, rows, width)

    pg_copies = [
        pltpu.make_async_remote_copy(
            src_ref=gwin.at[GRAD_SLOT[j] + 1 - core],
            dst_ref=from_partner.at[j],
            send_sem=pg_send.at[j],
            recv_sem=pg_recv.at[j],
            device_id=partner,
            device_id_type=MESH,
        )
        for j in range(5)
    ]
    og_copies = [
        pltpu.make_async_remote_copy(
            src_ref=out_bf.at[j],
            dst_ref=arrived.at[BACK[j]],
            send_sem=og_send.at[j],
            recv_sem=og_recv.at[BACK[j]],
            device_id=peer(hop),
            device_id_type=MESH,
        )
        for j, hop in enumerate(HOPS)
    ]

    def hand_out(which):
        for j in which:
            pg_copies[j].wait_recv()
            out_bf[j] = (gwin[GRAD_SLOT[j] + core] + from_partner[j]).astype(jnp.bfloat16)

            @pl.when(exists(HOPS[j]))
            def _(j=j):
                og_copies[j].start()

    gather(0, side_all)
    backproject(0, last_rows, 0, 4)
    pg_copies[0].start()
    pg_copies[2].start()
    gather(side_all, side_all)
    hand_out((0, 2))
    backproject(side_all, last_rows, 4, 4)
    pg_copies[1].start()
    pg_copies[3].start()
    gather(2 * side_all, tables * chip_rows)
    hand_out((1, 3))
    backproject(2 * side_all, chip_rows, 8, 2)
    pg_copies[4].start()

    @pl.when(has_below)
    def _():
        edge_copies[1].wait_recv()

    @pl.when(has_above)
    def _():
        edge_copies[0].wait_recv()

    here = vol_ref[...]
    row = lax.broadcasted_iota(jnp.int32, here.shape, 0)
    column = lax.broadcasted_iota(jnp.int32, here.shape, 1) % (plane // 2)

    def step_to(other, allowed):
        return jnp.where(allowed, jnp.clip(here - other, -DELTA, DELTA), 0.0)

    lower = jnp.where(row == 0, halo[0], pltpu.roll(here, 1, 0))
    upper = jnp.where(row == rows - 1, halo[1], pltpu.roll(here, rows - 1, 0))
    prior = step_to(lower, row + me > 0)
    prior = prior + step_to(upper, row + (me + 1 - n_dev) < rows - 1)
    prior = prior + jnp.clip(here - pltpu.roll(here, plane // 2, 1), -DELTA, DELTA)
    prior = prior + step_to(pltpu.roll(here, 1, 1), column > 0)
    prior = prior + step_to(pltpu.roll(here, plane - 1, 1), column < plane // 2 - 1)
    prior = PRIOR_WEIGHT * prior
    for piece in range(pieces):
        at_column = ((piece % 2) * (pieces // 2) + piece // 2) * 128
        prior_ref[pl.ds(piece, rows, stride=pieces), :] = prior[:, at_column : at_column + 128]

    pg_copies[4].wait_recv()
    total = gwin[8 + core] + from_partner[4]
    for j in range(4):

        @pl.when(exists(HOPS[j]))
        def _(j=j):
            og_copies[BACK[j]].wait_recv()

        total = total + arrived[j].astype(jnp.float32)
    for piece in range(pieces):
        at_column = ((piece % 2) * (pieces // 2) + piece // 2) * 128
        out_ref[pl.ds(piece, rows, stride=pieces), :] = total[:, at_column : at_column + 128]

    for j, hop in enumerate(HOPS):

        @pl.when(direct(hop))
        def _(j=j):
            vol_copies[j].wait_send()

        @pl.when(exists(hop))
        def _(j=j):
            pass_copies[j].wait_send()
            og_copies[j].wait_send()

    @pl.when(boxed)
    def _():
        box_copy.wait_send()

    @pl.when(relay)
    def _():
        fwd_copy.wait_send()

    @pl.when(tail)
    def _():
        step_copy.wait_send()

    pass_copies[4].wait_send()
    for j in range(5):
        pg_copies[j].wait_send()

    @pl.when(has_below)
    def _():
        edge_copies[0].wait_send()

    @pl.when(has_above)
    def _():
        edge_copies[1].wait_send()


def solution(mesh):
    n_grp, n_view = mesh.shape["grp"], mesh.shape["view"]

    def shards(volume, footprint, measured, angle_index, cover, offset, count):
        blocks, slab, strip, width = volume.shape
        views, det, channels = measured.shape
        tables = footprint.shape[0]
        rows, plane = blocks * slab, strip * width
        total_rows = tables * 5 * CORES * rows
        bf, f32 = jnp.bfloat16, jnp.float32
        dma = pltpu.SemaphoreType.DMA
        hbm = pl.BlockSpec(memory_space=pltpu.HBM)
        data, prior = pl.pallas_call(
            lambda *refs: kernel(n_grp, n_view, *refs),
            out_shape=[jax.ShapeDtypeStruct((rows * plane // 128, 128), f32)] * 2,
            in_specs=[hbm] * 7,
            out_specs=[pl.BlockSpec(memory_space=pltpu.VMEM)] * 2,
            scratch_shapes=[
                pltpu.SMEM(angle_index.shape, jnp.int32),
                pltpu.SMEM(cover.T.shape, jnp.int32),
                pltpu.SMEM(offset.T.shape, jnp.int32),
                pltpu.SMEM(count.shape, jnp.int32),
                pltpu.VMEM((rows * plane // 128, 128), f32),
                pltpu.VMEM((rows, plane), f32),
                pltpu.VMEM((tables, plane, channels), bf),
                pltpu.VMEM((views * det, channels), bf),
                pltpu.VMEM((views * det, channels), f32),
                pltpu.VMEM((10, rows, plane), bf),
                pltpu.VMEM((2, 1, plane), f32),
                pltpu.VMEM((2, 1, plane), f32),
                pltpu.VMEM((total_rows, views * det), bf),
                pltpu.VMEM((views * det, total_rows), bf),
                pltpu.VMEM((total_rows, channels), bf),
                pltpu.VMEM((total_rows, channels), bf),
                pltpu.VMEM((views * det, channels), f32),
                pltpu.VMEM((views * det, channels), bf),
                pltpu.VMEM((total_rows, channels), bf),
                pltpu.VMEM((10, rows, plane), f32),
                pltpu.VMEM((rows, plane), bf),
                pltpu.VMEM((5, rows, plane), f32),
                pltpu.VMEM((4, rows, plane), bf),
                pltpu.VMEM((4, rows, plane), bf),
                dma((7,)),
                dma((4,)),
                dma((4,)),
                dma((5,)),
                dma((5,)),
                dma((2,)),
                dma((2,)),
                dma((5,)),
                dma((5,)),
                dma((4,)),
                dma((4,)),
                dma((1,)),
                dma((1,)),
                dma((2,)),
                pltpu.SemaphoreType.REGULAR((1,)),
            ],
            compiler_params=pltpu.CompilerParams(
                collective_id=0, has_side_effects=True, vmem_limit_bytes=48 * 1024 * 1024
            ),
            name="ct_gradient",
        )(
            *(
                pltpu.with_memory_space_constraint(array, pltpu.HBM)
                for array in (
                    angle_index,
                    cover.T,
                    offset.T,
                    count,
                    volume.reshape(rows, strip, width // 128, 128).transpose(0, 2, 1, 3).reshape(-1, 128),
                    footprint.reshape(tables, plane, channels),
                    measured.reshape(views * det, channels),
                )
            )
        )
        gradient = data + prior
        return gradient.reshape(rows, width // 128, strip, 128).transpose(0, 2, 1, 3).reshape(volume.shape)

    axes = ("grp", "view")
    in_specs = (
        P(axes, None, None, None),
        P(axes, None, None, None),
        P(axes, None, None),
        P(axes),
        P(axes, None),
        P(axes, None),
        P(axes),
    )
    return jax.shard_map(
        shards, mesh=mesh, in_specs=in_specs, out_specs=P(axes, None, None, None), check_vma=False
    )
```

```python
import jax
import jax.numpy as jnp
from jax import lax
from jax.experimental import pallas as pl
from jax.experimental.pallas import tpu as pltpu
from jax.sharding import PartitionSpec as P

DELTA = 0.5
PRIOR_WEIGHT = 2.0
MESH = pl.DeviceIdType.MESH
HOPS = (1, -1, 2, -2)
BACK = (1, 0, 3, 2)
GRAD_SLOT = (0, 4, 2, 6, 8)
CORES = 2
LINE = 8
NT = (((1,), (1,)), ((), ()))


def chunks(total, width):
    return [(at, min(width, total - at)) for at in range(0, total, width)]


def kernel(
    n_grp,
    n_view,
    angle_hbm,
    cover_hbm,
    offset_hbm,
    count_hbm,
    vol_hbm,
    fp_hbm,
    meas_hbm,
    out_ref,
    prior_ref,
    angle_ref,
    cover_ref,
    offset_ref,
    count_ref,
    raw,
    vol_ref,
    fp,
    meas,
    gain,
    win,
    edge,
    halo,
    sel,
    sel_t,
    hi,
    proj,
    wres,
    gsum,
    gwin,
    box,
    from_partner,
    out_bf,
    arrived,
    load_sem,
    vol_send,
    vol_recv,
    pass_send,
    pass_recv,
    edge_send,
    edge_recv,
    pg_send,
    pg_recv,
    og_send,
    og_recv,
    box_send,
    box_recv,
    fwd_send,
    here_sem,
    gbox,
    gbox_send,
    gbox_recv,
    gfwd_send,
    gfwd_recv,
):
    n_dev = n_grp * n_view
    n_chip = n_dev // CORES
    me = lax.axis_index("grp") * n_view + lax.axis_index("view")
    chip = me // CORES
    core = me % CORES
    tables, plane, channels = fp.shape
    views = angle_ref.shape[0]
    slots = cover_ref.shape[0]
    rows = vol_ref.shape[0]
    slab = rows // 2
    pieces = plane // 128
    det = meas.shape[0] // views
    chip_rows = CORES * rows
    first_rows, last_rows = 3 * chip_rows, 2 * chip_rows
    first_all = tables * first_rows
    side_all = tables * last_rows
    total_rows = tables * 5 * chip_rows
    in_line = chip % LINE
    line = chip // LINE
    span = CORES * LINE
    line_below, line_above = line > 0, line < n_chip // LINE - 1

    def at(device):
        return (device // n_view, device % n_view)

    def exists(hop):
        return jnp.logical_and(chip + hop >= 0, chip + hop < n_chip)

    def peer(hop):
        return at(jnp.clip(me + CORES * hop, 0, n_dev - 1))

    partner = at(me + 1 - 2 * core)
    below, above = me - 1, me + 1
    has_below, has_above = below >= 0, above < n_dev

    def crosses(hop):
        return jnp.logical_or(in_line + hop < 0, in_line + hop >= LINE)

    def direct(hop):
        return jnp.logical_and(exists(hop), jnp.logical_not(crosses(hop))) if hop < 0 else exists(hop)

    relay = jnp.logical_and(in_line < 2, line_above)
    boxed = jnp.logical_and(in_line < 2, line_below)
    tail = jnp.logical_and(in_line == LINE - 1, line_above)
    to_tail = span - CORES * (1 + in_line)

    def device_at(offset):
        return at(jnp.clip(me + offset, 0, n_dev - 1))

    loads = [
        pltpu.make_async_copy(source, target, load_sem.at[n])
        for n, (source, target) in enumerate(
            (
                (vol_hbm, raw),
                (angle_hbm, angle_ref),
                (cover_hbm, cover_ref),
                (offset_hbm, offset_ref),
                (count_hbm, count_ref),
                (meas_hbm, meas),
                (fp_hbm, fp),
            )
        )
    ]
    for copy in loads[:5]:
        copy.start()

    barrier = pltpu.get_barrier_semaphore()
    expected = jnp.int32(1)

    def greet(allowed, offset, count=1):
        @pl.when(allowed)
        def _():
            pl.semaphore_signal(barrier, inc=count, device_id=device_at(offset), device_id_type=MESH)

    for hop in HOPS:
        if hop > 0:
            greet(jnp.logical_and(exists(hop), jnp.logical_not(crosses(hop))), CORES * hop)
        else:
            greet(exists(hop), CORES * hop)
        expected = expected + direct(hop).astype(jnp.int32)
    greet(relay, span)
    greet(relay, to_tail)
    expected = expected + boxed.astype(jnp.int32) + 2 * tail.astype(jnp.int32)
    pl.semaphore_signal(barrier, inc=1, device_id=partner, device_id_type=MESH)
    greet(jnp.logical_and(core == 0, has_below), -1)
    greet(jnp.logical_and(core == 1, jnp.logical_and(has_above, in_line < LINE - 1)), 1)
    expected = expected + jnp.logical_and(core == 1, has_above).astype(jnp.int32)
    expected = expected + jnp.logical_and(core == 0, in_line > 0).astype(jnp.int32)

    pl.semaphore_wait(barrier, expected)

    for offset in (CORES - span, 2 * CORES - span):

        @pl.when(tail)
        def _(offset=offset):
            pl.semaphore_signal(here_sem.at[0], inc=1, device_id=device_at(offset), device_id_type=MESH)

    loads[0].wait()
    for copy in loads[5:]:
        copy.start()
    for piece in range(pieces):
        at_column = ((piece % 2) * (pieces // 2) + piece // 2) * 128
        value = raw[pl.ds(piece, rows, stride=pieces), :]
        vol_ref[:, pl.ds(at_column, 128)] = value
        win[core, :, pl.ds(at_column, 128)] = value.astype(jnp.bfloat16)
    edge[0] = vol_ref[0:1, :]
    edge[1] = vol_ref[rows - 1 : rows, :]

    for j, hop in enumerate(HOPS):

        @pl.when(jnp.logical_not(exists(hop)))
        def _(j=j):
            win[2 + 2 * j] = jnp.zeros_like(win[2 + 2 * j])
            win[3 + 2 * j] = jnp.zeros_like(win[3 + 2 * j])
            arrived[j] = jnp.zeros_like(arrived[j])

    @pl.when(jnp.logical_not(has_below))
    def _():
        halo[0] = jnp.zeros_like(halo[0])

    @pl.when(jnp.logical_not(has_above))
    def _():
        halo[1] = jnp.zeros_like(halo[1])


    vol_copies = [
        pltpu.make_async_remote_copy(
            src_ref=win.at[core],
            dst_ref=win.at[2 + 2 * BACK[j] + core],
            send_sem=vol_send.at[j],
            recv_sem=vol_recv.at[BACK[j]],
            device_id=peer(hop),
            device_id_type=MESH,
        )
        for j, hop in enumerate(HOPS)
    ]
    box_copy = pltpu.make_async_remote_copy(
        src_ref=win.at[core],
        dst_ref=box,
        send_sem=box_send.at[0],
        recv_sem=box_recv.at[0],
        device_id=device_at(-span),
        device_id_type=MESH,
    )
    fwd_copy = pltpu.make_async_remote_copy(
        src_ref=box,
        dst_ref=win.at[2 + 4 * in_line + core],
        send_sem=fwd_send.at[0],
        recv_sem=vol_recv.at[2 * in_line],
        device_id=device_at(to_tail),
        device_id_type=MESH,
    )
    step_copy = pltpu.make_async_remote_copy(
        src_ref=win.at[2 + core],
        dst_ref=win.at[6 + core],
        send_sem=fwd_send.at[1],
        recv_sem=vol_recv.at[2],
        device_id=device_at(-CORES),
        device_id_type=MESH,
    )
    window_slot = [2 + 2 * j for j in range(4)] + [0]
    pass_copies = [
        pltpu.make_async_remote_copy(
            src_ref=win.at[slot + core],
            dst_ref=win.at[slot + core],
            send_sem=pass_send.at[j],
            recv_sem=pass_recv.at[j],
            device_id=partner,
            device_id_type=MESH,
        )
        for j, slot in enumerate(window_slot)
    ]
    edge_copies = [
        pltpu.make_async_remote_copy(
            src_ref=edge.at[side],
            dst_ref=halo.at[1 - side],
            send_sem=edge_send.at[side],
            recv_sem=edge_recv.at[1 - side],
            device_id=device_at(2 * side - 1),
            device_id_type=MESH,
        )
        for side in range(2)
    ]

    @pl.when(boxed)
    def _():
        box_copy.start()

    for j in range(4):

        @pl.when(direct(HOPS[j]))
        def _(j=j):
            vol_copies[j].start()

    pass_copies[4].start()
    edge_waits = jnp.logical_and(core == 0, in_line == 0)

    @pl.when(jnp.logical_and(has_below, jnp.logical_not(edge_waits)))
    def _():
        edge_copies[0].start()

    @pl.when(has_above)
    def _():
        edge_copies[1].start()

    for copy in loads[1:5]:
        copy.wait()

    first_block = (chip - 2) * 4
    row_of = []
    for v in range(views):
        here = []
        for k in range(slots):
            block = cover_ref[k, v] - first_block
            distance = block // 4 - 2
            reach = jnp.abs(distance)
            within = (block % 4) * slab
            table = angle_ref[v]
            off = offset_ref[k, v]
            under = jnp.where(distance < 0, 1, 0)
            place = jnp.where(reach == 0, 0, 2 * reach - 1 + under) * chip_rows + within
            ahead = jnp.where(
                reach < 2, table * first_rows + place, first_all + table * last_rows + place - first_rows
            )
            side = under * side_all + table * last_rows + (reach - 1) * chip_rows + within
            behind = jnp.where(reach > 0, side, 2 * side_all + table * chip_rows + within)
            here.append((ahead - off, behind - off, off, k < count_ref[v]))
        row_of.append(here)

    det_iota = lax.broadcasted_iota(jnp.int32, (det, 128), 0)
    for v in range(views):
        goals = []
        for row, _, off, live in row_of[v]:
            off_live = jnp.where(live, off, -4096)
            inside = jnp.logical_and(det_iota >= off_live, det_iota < off_live + slab)
            goals.append(jnp.where(inside, det_iota + row, -1))
        for tile in range(total_rows // 128):
            lane = lax.broadcasted_iota(jnp.int32, (det, 128), 1) + tile * 128
            hits = jnp.zeros((det, 128), jnp.float32)
            for goal in goals:
                hits = hits + jnp.where(goal == lane, 1.0, 0.0)
            sel_t[pl.ds(v * det, det), pl.ds(tile * 128, 128)] = hits.astype(jnp.bfloat16)
    lane = lax.broadcasted_iota(jnp.int32, (8, views * det), 1)
    goals = []
    for k in range(slots):
        goal = jnp.full((8, views * det), -1, jnp.int32)
        for v in range(views):
            _, row, off, live = row_of[v][k]
            off_live = jnp.where(live, off, -4096)
            spot = lane - v * det
            inside = jnp.logical_and(
                jnp.logical_and(spot >= off_live, spot < off_live + slab),
                jnp.logical_and(spot >= 0, spot < det),
            )
            goal = jnp.where(inside, spot + row, goal)
        goals.append(goal[0:1, :])

    def build_sel(step, _):
        at_row = pl.multiple_of(step * 32, 32)
        index = lax.broadcasted_iota(jnp.int32, (32, views * det), 0) + step * 32
        hits = jnp.zeros((32, views * det), jnp.float32)
        for goal in goals:
            hits = hits + jnp.where(goal == index, 1.0, 0.0)
        sel[pl.ds(at_row, 32), :] = hits.astype(jnp.bfloat16)
        return 0

    lax.fori_loop(0, total_rows // 32, build_sel, 0)

    loads[5].wait()

    def build_gain(step, _):
        part = pl.ds(pl.multiple_of(step * 32, 32), 32)
        gain[part, :] = jnp.exp(-meas[part, :].astype(jnp.float32))
        return 0

    lax.fori_loop(0, meas.shape[0] // 32, build_gain, 0)
    loads[6].wait()

    def project(first_slot, slot_count, first_row):
        block = win[pl.ds(first_slot, slot_count)].reshape(slot_count * rows, plane)
        height = slot_count * rows
        for table in range(tables):
            for start, width in chunks(channels, 256):
                cols = pl.ds(start, width)
                product = jnp.dot(block, fp[table, :, cols], preferred_element_type=jnp.float32)
                hi[pl.ds(first_row + table * height, height), cols] = product.astype(jnp.bfloat16)

    def placed(first_row, height, cols):
        pick = sel_t[:, pl.ds(first_row, height)]
        part = pl.ds(first_row, height)
        return jnp.dot(pick, hi[part, cols], preferred_element_type=jnp.float32)

    def collect(which):
        for j in which:

            @pl.when(exists(HOPS[j]))
            def _(j=j):
                vol_copies[BACK[j]].wait_recv()
                pass_copies[j].start()

            if j == 0:

                @pl.when(tail)
                def _():
                    step_copy.start()

        for j in which:

            @pl.when(exists(HOPS[j]))
            def _(j=j):
                pass_copies[j].wait_recv()

    @pl.when(relay)
    def _():
        box_copy.wait_recv()
        pl.semaphore_wait(here_sem.at[0], 1)
        fwd_copy.start()

    pass_copies[4].wait_recv()
    collect((0, 1))

    @pl.when(jnp.logical_and(has_below, edge_waits))
    def _():
        edge_copies[0].start()

    project(0, 6, 0)
    for start, width in chunks(channels, 256):
        cols = pl.ds(start, width)
        proj[:, cols] = placed(0, first_all, cols)
    collect((2, 3))
    project(6, 4, first_all)
    for start, width in chunks(channels, 256):
        cols = pl.ds(start, width)
        forward = proj[:, cols] + placed(first_all, side_all, cols)
        wres[:, cols] = (gain[:, cols] * (forward - meas[:, cols].astype(jnp.float32))).astype(jnp.bfloat16)

    def gather(first_row, height):
        part = pl.ds(first_row, height)
        for start, width in chunks(channels, 256):
            cols = pl.ds(start, width)
            gsum[part, cols] = jnp.dot(sel[part, :], wres[:, cols], preferred_element_type=jnp.float32).astype(
                jnp.bfloat16
            )

    def backproject(first_row, stride, first_slot, slot_count):
        height = slot_count * rows
        for start, width in chunks(plane, 256):
            total = None
            for table in range(tables):
                term = lax.dot_general(
                    gsum[pl.ds(first_row + table * stride, height), :],
                    fp[table, pl.ds(start, width), :],
                    NT,
                    preferred_element_type=jnp.float32,
                )
                total = term if total is None else total + term
            gwin[pl.ds(first_slot, slot_count), :, pl.ds(start, width)] = total.reshape(slot_count, rows, width)

    pg_copies = [
        pltpu.make_async_remote_copy(
            src_ref=gwin.at[GRAD_SLOT[j] + 1 - core],
            dst_ref=from_partner.at[j],
            send_sem=pg_send.at[j],
            recv_sem=pg_recv.at[j],
            device_id=partner,
            device_id_type=MESH,
        )
        for j in range(5)
    ]
    og_copies = [
        pltpu.make_async_remote_copy(
            src_ref=out_bf.at[j],
            dst_ref=arrived.at[BACK[j]],
            send_sem=og_send.at[j],
            recv_sem=og_recv.at[BACK[j]],
            device_id=peer(hop),
            device_id_type=MESH,
        )
        for j, hop in enumerate(HOPS)
    ]

    half = rows // 2
    og_half = pltpu.make_async_remote_copy(
        src_ref=out_bf.at[2, pl.ds(0, half)],
        dst_ref=arrived.at[3, pl.ds(0, half)],
        send_sem=og_send.at[2],
        recv_sem=og_recv.at[3],
        device_id=peer(HOPS[2]),
        device_id_type=MESH,
    )
    gbox_copy = pltpu.make_async_remote_copy(
        src_ref=out_bf.at[2, pl.ds(half, half)],
        dst_ref=gbox,
        send_sem=gbox_send.at[0],
        recv_sem=gbox_recv.at[0],
        device_id=device_at(2 * CORES - span),
        device_id_type=MESH,
    )
    gfwd_copy = pltpu.make_async_remote_copy(
        src_ref=gbox,
        dst_ref=arrived.at[3, pl.ds(half, half)],
        send_sem=gfwd_send.at[0],
        recv_sem=gfwd_recv.at[0],
        device_id=device_at(span),
        device_id_type=MESH,
    )
    second = in_line == 1
    gives_half = jnp.logical_and(second, line_above)
    takes_half = jnp.logical_and(second, line_below)

    def whole(j):
        return jnp.logical_and(exists(HOPS[j]), jnp.logical_not(tail)) if j == 2 else exists(HOPS[j])

    def hand_out(which):
        for j in which:
            pg_copies[j].wait_recv()
            out_bf[j] = (gwin[GRAD_SLOT[j] + core] + from_partner[j]).astype(jnp.bfloat16)

            @pl.when(whole(j))
            def _(j=j):
                og_copies[j].start()

            if j == 2:

                @pl.when(tail)
                def _():
                    gbox_copy.start()
                    og_half.start()

    gather(0, side_all)
    backproject(0, last_rows, 0, 4)
    pg_copies[0].start()
    pg_copies[2].start()
    gather(side_all, side_all)
    hand_out((0, 2))
    backproject(side_all, last_rows, 4, 4)
    pg_copies[1].start()
    pg_copies[3].start()
    gather(2 * side_all, tables * chip_rows)
    hand_out((1, 3))
    backproject(2 * side_all, chip_rows, 8, 2)
    pg_copies[4].start()

    @pl.when(has_below)
    def _():
        edge_copies[1].wait_recv()

    @pl.when(has_above)
    def _():
        edge_copies[0].wait_recv()

    here = vol_ref[...]
    row = lax.broadcasted_iota(jnp.int32, here.shape, 0)
    column = lax.broadcasted_iota(jnp.int32, here.shape, 1) % (plane // 2)

    def step_to(other, allowed):
        return jnp.where(allowed, jnp.clip(here - other, -DELTA, DELTA), 0.0)

    lower = jnp.where(row == 0, halo[0], pltpu.roll(here, 1, 0))
    upper = jnp.where(row == rows - 1, halo[1], pltpu.roll(here, rows - 1, 0))
    prior = step_to(lower, row + me > 0)
    prior = prior + step_to(upper, row + (me + 1 - n_dev) < rows - 1)
    prior = prior + jnp.clip(here - pltpu.roll(here, plane // 2, 1), -DELTA, DELTA)
    prior = prior + step_to(pltpu.roll(here, 1, 1), column > 0)
    prior = prior + step_to(pltpu.roll(here, plane - 1, 1), column < plane // 2 - 1)
    prior = PRIOR_WEIGHT * prior
    for piece in range(pieces):
        at_column = ((piece % 2) * (pieces // 2) + piece // 2) * 128
        prior_ref[pl.ds(piece, rows, stride=pieces), :] = prior[:, at_column : at_column + 128]

    @pl.when(gives_half)
    def _():
        gbox_copy.wait_recv()
        gfwd_copy.start()

    pg_copies[4].wait_recv()
    total = gwin[8 + core] + from_partner[4]
    for j in range(4):

        comes = exists(HOPS[j])
        if j == 3:
            comes = jnp.logical_and(comes, jnp.logical_not(takes_half))

            @pl.when(takes_half)
            def _():
                og_half.wait_recv()
                gfwd_copy.wait_recv()

        @pl.when(comes)
        def _(j=j):
            og_copies[BACK[j]].wait_recv()

        total = total + arrived[j].astype(jnp.float32)
    for piece in range(pieces):
        at_column = ((piece % 2) * (pieces // 2) + piece // 2) * 128
        out_ref[pl.ds(piece, rows, stride=pieces), :] = total[:, at_column : at_column + 128]

    for j, hop in enumerate(HOPS):

        @pl.when(direct(hop))
        def _(j=j):
            vol_copies[j].wait_send()

        @pl.when(exists(hop))
        def _(j=j):
            pass_copies[j].wait_send()

        @pl.when(whole(j))
        def _(j=j):
            og_copies[j].wait_send()

    @pl.when(tail)
    def _():
        og_half.wait_send()
        gbox_copy.wait_send()

    @pl.when(gives_half)
    def _():
        gfwd_copy.wait_send()

    @pl.when(boxed)
    def _():
        box_copy.wait_send()

    @pl.when(relay)
    def _():
        fwd_copy.wait_send()

    @pl.when(tail)
    def _():
        step_copy.wait_send()

    pass_copies[4].wait_send()
    for j in range(5):
        pg_copies[j].wait_send()

    @pl.when(has_below)
    def _():
        edge_copies[0].wait_send()

    @pl.when(has_above)
    def _():
        edge_copies[1].wait_send()


def solution(mesh):
    n_grp, n_view = mesh.shape["grp"], mesh.shape["view"]

    def shards(volume, footprint, measured, angle_index, cover, offset, count):
        blocks, slab, strip, width = volume.shape
        views, det, channels = measured.shape
        tables = footprint.shape[0]
        rows, plane = blocks * slab, strip * width
        total_rows = tables * 5 * CORES * rows
        bf, f32 = jnp.bfloat16, jnp.float32
        dma = pltpu.SemaphoreType.DMA
        hbm = pl.BlockSpec(memory_space=pltpu.HBM)
        data, prior = pl.pallas_call(
            lambda *refs: kernel(n_grp, n_view, *refs),
            out_shape=[jax.ShapeDtypeStruct((rows * plane // 128, 128), f32)] * 2,
            in_specs=[hbm] * 7,
            out_specs=[pl.BlockSpec(memory_space=pltpu.VMEM)] * 2,
            scratch_shapes=[
                pltpu.SMEM(angle_index.shape, jnp.int32),
                pltpu.SMEM(cover.T.shape, jnp.int32),
                pltpu.SMEM(offset.T.shape, jnp.int32),
                pltpu.SMEM(count.shape, jnp.int32),
                pltpu.VMEM((rows * plane // 128, 128), f32),
                pltpu.VMEM((rows, plane), f32),
                pltpu.VMEM((tables, plane, channels), bf),
                pltpu.VMEM((views * det, channels), bf),
                pltpu.VMEM((views * det, channels), f32),
                pltpu.VMEM((10, rows, plane), bf),
                pltpu.VMEM((2, 1, plane), f32),
                pltpu.VMEM((2, 1, plane), f32),
                pltpu.VMEM((total_rows, views * det), bf),
                pltpu.VMEM((views * det, total_rows), bf),
                pltpu.VMEM((total_rows, channels), bf),
                pltpu.VMEM((views * det, channels), f32),
                pltpu.VMEM((views * det, channels), bf),
                pltpu.VMEM((total_rows, channels), bf),
                pltpu.VMEM((10, rows, plane), f32),
                pltpu.VMEM((rows, plane), bf),
                pltpu.VMEM((5, rows, plane), f32),
                pltpu.VMEM((4, rows, plane), bf),
                pltpu.VMEM((4, rows, plane), bf),
                dma((7,)),
                dma((4,)),
                dma((4,)),
                dma((5,)),
                dma((5,)),
                dma((2,)),
                dma((2,)),
                dma((5,)),
                dma((5,)),
                dma((4,)),
                dma((4,)),
                dma((1,)),
                dma((1,)),
                dma((2,)),
                pltpu.SemaphoreType.REGULAR((1,)),
                pltpu.VMEM((rows // 2, plane), bf),
                dma((1,)),
                dma((1,)),
                dma((1,)),
                dma((1,)),
            ],
            compiler_params=pltpu.CompilerParams(
                collective_id=0, has_side_effects=True, vmem_limit_bytes=48 * 1024 * 1024
            ),
            name="ct_gradient",
        )(
            *(
                pltpu.with_memory_space_constraint(array, pltpu.HBM)
                for array in (
                    angle_index,
                    cover.T,
                    offset.T,
                    count,
                    volume.reshape(rows, strip, width // 128, 128).transpose(0, 2, 1, 3).reshape(-1, 128),
                    footprint.reshape(tables, plane, channels),
                    measured.reshape(views * det, channels),
                )
            )
        )
        gradient = data + prior
        return gradient.reshape(rows, width // 128, strip, 128).transpose(0, 2, 1, 3).reshape(volume.shape)

    axes = ("grp", "view")
    in_specs = (
        P(axes, None, None, None),
        P(axes, None, None, None),
        P(axes, None, None),
        P(axes),
        P(axes, None),
        P(axes, None),
        P(axes),
    )
    return jax.shard_map(
        shards, mesh=mesh, in_specs=in_specs, out_specs=P(axes, None, None, None), check_vma=False
    )
```

```python
import jax
import jax.numpy as jnp
from jax import lax
from jax.experimental import pallas as pl
from jax.experimental.pallas import tpu as pltpu
from jax.sharding import PartitionSpec as P

DELTA = 0.5
PRIOR_WEIGHT = 2.0
MESH = pl.DeviceIdType.MESH
HOPS = (1, -1, 2, -2)
BACK = (1, 0, 3, 2)
GRAD_SLOT = (0, 4, 2, 6, 8)
CORES = 2
LINE = 8
NT = (((1,), (1,)), ((), ()))


def chunks(total, width):
    return [(at, min(width, total - at)) for at in range(0, total, width)]


def kernel(
    n_grp,
    n_view,
    angle_hbm,
    cover_hbm,
    offset_hbm,
    count_hbm,
    vol_hbm,
    fp_hbm,
    meas_hbm,
    out_ref,
    prior_ref,
    angle_ref,
    cover_ref,
    offset_ref,
    count_ref,
    raw,
    vol_ref,
    fp,
    meas,
    gain,
    win,
    edge,
    halo,
    sel,
    sel_t,
    hi,
    proj,
    wres,
    gsum,
    gwin,
    box,
    from_partner,
    out_bf,
    arrived,
    load_sem,
    vol_send,
    vol_recv,
    pass_send,
    pass_recv,
    edge_send,
    edge_recv,
    pg_send,
    pg_recv,
    og_send,
    og_recv,
    box_send,
    box_recv,
    fwd_send,
    here_sem,
    up_sem,
    gbox,
    gbox_send,
    gbox_recv,
    gfwd_send,
    gfwd_recv,
):
    n_dev = n_grp * n_view
    n_chip = n_dev // CORES
    me = lax.axis_index("grp") * n_view + lax.axis_index("view")
    chip = me // CORES
    core = me % CORES
    tables, plane, channels = fp.shape
    views = angle_ref.shape[0]
    slots = cover_ref.shape[0]
    rows = vol_ref.shape[0]
    slab = rows // 2
    pieces = plane // 128
    det = meas.shape[0] // views
    chip_rows = CORES * rows
    first_rows, last_rows = 3 * chip_rows, 2 * chip_rows
    first_all = tables * first_rows
    side_all = tables * last_rows
    total_rows = tables * 5 * chip_rows
    in_line = chip % LINE
    line = chip // LINE
    span = CORES * LINE
    line_below, line_above = line > 0, line < n_chip // LINE - 1

    def at(device):
        return (device // n_view, device % n_view)

    def exists(hop):
        return jnp.logical_and(chip + hop >= 0, chip + hop < n_chip)

    def peer(hop):
        return at(jnp.clip(me + CORES * hop, 0, n_dev - 1))

    partner = at(me + 1 - 2 * core)
    below, above = me - 1, me + 1
    has_below, has_above = below >= 0, above < n_dev

    def crosses(hop):
        return jnp.logical_or(in_line + hop < 0, in_line + hop >= LINE)

    def direct(hop):
        return jnp.logical_and(exists(hop), jnp.logical_not(crosses(hop))) if hop < 0 else exists(hop)

    relay = jnp.logical_and(in_line < 2, line_above)
    boxed = jnp.logical_and(in_line < 2, line_below)
    tail = jnp.logical_and(in_line == LINE - 1, line_above)
    to_tail = span - CORES * (1 + in_line)

    def device_at(offset):
        return at(jnp.clip(me + offset, 0, n_dev - 1))

    loads = [
        pltpu.make_async_copy(source, target, load_sem.at[n])
        for n, (source, target) in enumerate(
            (
                (vol_hbm, raw),
                (angle_hbm, angle_ref),
                (cover_hbm, cover_ref),
                (offset_hbm, offset_ref),
                (count_hbm, count_ref),
                (meas_hbm, meas),
                (fp_hbm, fp),
            )
        )
    ]
    for copy in loads[:5]:
        copy.start()

    barrier = pltpu.get_barrier_semaphore()
    expected = jnp.int32(1)

    def greet(allowed, offset, count=1):
        @pl.when(allowed)
        def _():
            pl.semaphore_signal(barrier, inc=count, device_id=device_at(offset), device_id_type=MESH)

    for hop in HOPS:
        inside = jnp.logical_and(exists(hop), jnp.logical_not(crosses(hop)))
        beyond = jnp.logical_and(exists(hop), crosses(hop))
        greet(inside if hop > 0 else beyond, CORES * hop)
        expected = expected + (inside if hop < 0 else beyond).astype(jnp.int32)
    greet(relay, span)
    greet(relay, to_tail)
    expected = expected + boxed.astype(jnp.int32) + 2 * tail.astype(jnp.int32)
    pl.semaphore_signal(barrier, inc=1, device_id=partner, device_id_type=MESH)
    pl.semaphore_wait(barrier, expected)

    for offset in (CORES - span, 2 * CORES - span):

        @pl.when(tail)
        def _(offset=offset):
            pl.semaphore_signal(here_sem.at[0], inc=1, device_id=device_at(offset), device_id_type=MESH)

    for hop in (-1, -2):

        @pl.when(direct(hop))
        def _(hop=hop):
            pl.semaphore_signal(
                up_sem.at[-hop - 1], inc=1, device_id=device_at(CORES * hop), device_id_type=MESH
            )

    loads[0].wait()
    for copy in loads[5:]:
        copy.start()
    for piece in range(pieces):
        at_column = ((piece % 2) * (pieces // 2) + piece // 2) * 128
        value = raw[pl.ds(piece, rows, stride=pieces), :]
        vol_ref[:, pl.ds(at_column, 128)] = value
        win[core, :, pl.ds(at_column, 128)] = value.astype(jnp.bfloat16)
    edge[0] = vol_ref[0:1, :]
    edge[1] = vol_ref[rows - 1 : rows, :]

    for j, hop in enumerate(HOPS):

        @pl.when(jnp.logical_not(exists(hop)))
        def _(j=j):
            win[2 + 2 * j] = jnp.zeros_like(win[2 + 2 * j])
            win[3 + 2 * j] = jnp.zeros_like(win[3 + 2 * j])
            arrived[j] = jnp.zeros_like(arrived[j])

    @pl.when(jnp.logical_not(has_below))
    def _():
        halo[0] = jnp.zeros_like(halo[0])

    @pl.when(jnp.logical_not(has_above))
    def _():
        halo[1] = jnp.zeros_like(halo[1])


    vol_copies = [
        pltpu.make_async_remote_copy(
            src_ref=win.at[core],
            dst_ref=win.at[2 + 2 * BACK[j] + core],
            send_sem=vol_send.at[j],
            recv_sem=vol_recv.at[BACK[j]],
            device_id=peer(hop),
            device_id_type=MESH,
        )
        for j, hop in enumerate(HOPS)
    ]
    box_copy = pltpu.make_async_remote_copy(
        src_ref=win.at[core],
        dst_ref=box,
        send_sem=box_send.at[0],
        recv_sem=box_recv.at[0],
        device_id=device_at(-span),
        device_id_type=MESH,
    )
    fwd_copy = pltpu.make_async_remote_copy(
        src_ref=box,
        dst_ref=win.at[2 + 4 * in_line + core],
        send_sem=fwd_send.at[0],
        recv_sem=vol_recv.at[2 * in_line],
        device_id=device_at(to_tail),
        device_id_type=MESH,
    )
    step_copy = pltpu.make_async_remote_copy(
        src_ref=win.at[2 + core],
        dst_ref=win.at[6 + core],
        send_sem=fwd_send.at[1],
        recv_sem=vol_recv.at[2],
        device_id=device_at(-CORES),
        device_id_type=MESH,
    )
    window_slot = [2 + 2 * j for j in range(4)] + [0]
    pass_copies = [
        pltpu.make_async_remote_copy(
            src_ref=win.at[slot + core],
            dst_ref=win.at[slot + core],
            send_sem=pass_send.at[j],
            recv_sem=pass_recv.at[j],
            device_id=partner,
            device_id_type=MESH,
        )
        for j, slot in enumerate(window_slot)
    ]
    edge_copies = [
        pltpu.make_async_remote_copy(
            src_ref=edge.at[side],
            dst_ref=halo.at[1 - side],
            send_sem=edge_send.at[side],
            recv_sem=edge_recv.at[1 - side],
            device_id=device_at(2 * side - 1),
            device_id_type=MESH,
        )
        for side in range(2)
    ]

    @pl.when(boxed)
    def _():
        box_copy.start()

    for j in (1, 3):

        @pl.when(direct(HOPS[j]))
        def _(j=j):
            vol_copies[j].start()

    pass_copies[4].start()
    for j in (0, 2):

        @pl.when(jnp.logical_and(exists(HOPS[j]), jnp.logical_not(crosses(HOPS[j]))))
        def _(j=j):
            pl.semaphore_wait(up_sem.at[HOPS[j] - 1], 1)

        @pl.when(exists(HOPS[j]))
        def _(j=j):
            vol_copies[j].start()

    for copy in loads[1:5]:
        copy.wait()

    first_block = (chip - 2) * 4
    row_of = []
    for v in range(views):
        here = []
        for k in range(slots):
            block = cover_ref[k, v] - first_block
            distance = block // 4 - 2
            reach = jnp.abs(distance)
            within = (block % 4) * slab
            table = angle_ref[v]
            off = offset_ref[k, v]
            under = jnp.where(distance < 0, 1, 0)
            place = jnp.where(reach == 0, 0, 2 * reach - 1 + under) * chip_rows + within
            ahead = jnp.where(
                reach < 2, table * first_rows + place, first_all + table * last_rows + place - first_rows
            )
            side = under * side_all + table * last_rows + (reach - 1) * chip_rows + within
            behind = jnp.where(reach > 0, side, 2 * side_all + table * chip_rows + within)
            here.append((ahead - off, behind - off, off, k < count_ref[v]))
        row_of.append(here)

    det_iota = lax.broadcasted_iota(jnp.int32, (det, 128), 0)
    for v in range(views):
        goals = []
        for row, _, off, live in row_of[v]:
            off_live = jnp.where(live, off, -4096)
            inside = jnp.logical_and(det_iota >= off_live, det_iota < off_live + slab)
            goals.append(jnp.where(inside, det_iota + row, -1))
        for tile in range(total_rows // 128):
            lane = lax.broadcasted_iota(jnp.int32, (det, 128), 1) + tile * 128
            hits = jnp.zeros((det, 128), jnp.float32)
            for goal in goals:
                hits = hits + jnp.where(goal == lane, 1.0, 0.0)
            sel_t[pl.ds(v * det, det), pl.ds(tile * 128, 128)] = hits.astype(jnp.bfloat16)
    lane = lax.broadcasted_iota(jnp.int32, (8, views * det), 1)
    goals = []
    for k in range(slots):
        goal = jnp.full((8, views * det), -1, jnp.int32)
        for v in range(views):
            _, row, off, live = row_of[v][k]
            off_live = jnp.where(live, off, -4096)
            spot = lane - v * det
            inside = jnp.logical_and(
                jnp.logical_and(spot >= off_live, spot < off_live + slab),
                jnp.logical_and(spot >= 0, spot < det),
            )
            goal = jnp.where(inside, spot + row, goal)
        goals.append(goal[0:1, :])

    def build_sel(step, _):
        at_row = pl.multiple_of(step * 32, 32)
        index = lax.broadcasted_iota(jnp.int32, (32, views * det), 0) + step * 32
        hits = jnp.zeros((32, views * det), jnp.float32)
        for goal in goals:
            hits = hits + jnp.where(goal == index, 1.0, 0.0)
        sel[pl.ds(at_row, 32), :] = hits.astype(jnp.bfloat16)
        return 0

    lax.fori_loop(0, total_rows // 32, build_sel, 0)

    loads[5].wait()

    def build_gain(step, _):
        part = pl.ds(pl.multiple_of(step * 32, 32), 32)
        gain[part, :] = jnp.exp(-meas[part, :].astype(jnp.float32))
        return 0

    lax.fori_loop(0, meas.shape[0] // 32, build_gain, 0)
    loads[6].wait()

    def project(first_slot, slot_count, first_row):
        block = win[pl.ds(first_slot, slot_count)].reshape(slot_count * rows, plane)
        height = slot_count * rows
        for table in range(tables):
            for start, width in chunks(channels, 256):
                cols = pl.ds(start, width)
                product = jnp.dot(block, fp[table, :, cols], preferred_element_type=jnp.float32)
                hi[pl.ds(first_row + table * height, height), cols] = product.astype(jnp.bfloat16)

    def placed(first_row, height, cols):
        pick = sel_t[:, pl.ds(first_row, height)]
        part = pl.ds(first_row, height)
        return jnp.dot(pick, hi[part, cols], preferred_element_type=jnp.float32)

    def collect(which):
        for j in which:

            @pl.when(exists(HOPS[j]))
            def _(j=j):
                vol_copies[BACK[j]].wait_recv()
                pass_copies[j].start()

            if j == 0:

                @pl.when(tail)
                def _():
                    step_copy.start()

        for j in which:

            @pl.when(exists(HOPS[j]))
            def _(j=j):
                pass_copies[j].wait_recv()

    @pl.when(relay)
    def _():
        box_copy.wait_recv()
        pl.semaphore_wait(here_sem.at[0], 1)
        fwd_copy.start()

    pass_copies[4].wait_recv()
    collect((0, 1))

    @pl.when(has_below)
    def _():
        edge_copies[0].start()

    @pl.when(has_above)
    def _():
        edge_copies[1].start()

    project(0, 6, 0)
    for start, width in chunks(channels, 256):
        cols = pl.ds(start, width)
        proj[:, cols] = placed(0, first_all, cols)
    collect((2, 3))
    project(6, 4, first_all)
    for start, width in chunks(channels, 256):
        cols = pl.ds(start, width)
        forward = proj[:, cols] + placed(first_all, side_all, cols)
        wres[:, cols] = (gain[:, cols] * (forward - meas[:, cols].astype(jnp.float32))).astype(jnp.bfloat16)

    def gather(first_row, height):
        part = pl.ds(first_row, height)
        for start, width in chunks(channels, 256):
            cols = pl.ds(start, width)
            gsum[part, cols] = jnp.dot(sel[part, :], wres[:, cols], preferred_element_type=jnp.float32).astype(
                jnp.bfloat16
            )

    def backproject(first_row, stride, first_slot, slot_count):
        height = slot_count * rows
        for start, width in chunks(plane, 256):
            total = None
            for table in range(tables):
                term = lax.dot_general(
                    gsum[pl.ds(first_row + table * stride, height), :],
                    fp[table, pl.ds(start, width), :],
                    NT,
                    preferred_element_type=jnp.float32,
                )
                total = term if total is None else total + term
            gwin[pl.ds(first_slot, slot_count), :, pl.ds(start, width)] = total.reshape(slot_count, rows, width)

    pg_copies = [
        pltpu.make_async_remote_copy(
            src_ref=gwin.at[GRAD_SLOT[j] + 1 - core],
            dst_ref=from_partner.at[j],
            send_sem=pg_send.at[j],
            recv_sem=pg_recv.at[j],
            device_id=partner,
            device_id_type=MESH,
        )
        for j in range(5)
    ]
    og_copies = [
        pltpu.make_async_remote_copy(
            src_ref=out_bf.at[j],
            dst_ref=arrived.at[BACK[j]],
            send_sem=og_send.at[j],
            recv_sem=og_recv.at[BACK[j]],
            device_id=peer(hop),
            device_id_type=MESH,
        )
        for j, hop in enumerate(HOPS)
    ]

    half = rows // 2
    og_half = pltpu.make_async_remote_copy(
        src_ref=out_bf.at[2, pl.ds(0, half)],
        dst_ref=arrived.at[3, pl.ds(0, half)],
        send_sem=og_send.at[2],
        recv_sem=og_recv.at[3],
        device_id=peer(HOPS[2]),
        device_id_type=MESH,
    )
    gbox_copy = pltpu.make_async_remote_copy(
        src_ref=out_bf.at[2, pl.ds(half, half)],
        dst_ref=gbox,
        send_sem=gbox_send.at[0],
        recv_sem=gbox_recv.at[0],
        device_id=device_at(2 * CORES - span),
        device_id_type=MESH,
    )
    gfwd_copy = pltpu.make_async_remote_copy(
        src_ref=gbox,
        dst_ref=arrived.at[3, pl.ds(half, half)],
        send_sem=gfwd_send.at[0],
        recv_sem=gfwd_recv.at[0],
        device_id=device_at(span),
        device_id_type=MESH,
    )
    second = in_line == 1
    gives_half = jnp.logical_and(second, line_above)
    takes_half = jnp.logical_and(second, line_below)

    def whole(j):
        return jnp.logical_and(exists(HOPS[j]), jnp.logical_not(tail)) if j == 2 else exists(HOPS[j])

    def hand_out(which):
        for j in which:
            pg_copies[j].wait_recv()
            out_bf[j] = (gwin[GRAD_SLOT[j] + core] + from_partner[j]).astype(jnp.bfloat16)

            @pl.when(whole(j))
            def _(j=j):
                og_copies[j].start()

            if j == 2:

                @pl.when(tail)
                def _():
                    gbox_copy.start()
                    og_half.start()

    gather(0, side_all)
    backproject(0, last_rows, 0, 4)
    pg_copies[0].start()
    pg_copies[2].start()
    gather(side_all, side_all)
    backproject(side_all, last_rows, 4, 4)
    pg_copies[1].start()
    pg_copies[3].start()
    hand_out((0, 2))
    gather(2 * side_all, tables * chip_rows)
    hand_out((1, 3))
    backproject(2 * side_all, chip_rows, 8, 2)
    pg_copies[4].start()

    @pl.when(has_below)
    def _():
        edge_copies[1].wait_recv()

    @pl.when(has_above)
    def _():
        edge_copies[0].wait_recv()

    here = vol_ref[...]
    row = lax.broadcasted_iota(jnp.int32, here.shape, 0)
    column = lax.broadcasted_iota(jnp.int32, here.shape, 1) % (plane // 2)

    def step_to(other, allowed):
        return jnp.where(allowed, jnp.clip(here - other, -DELTA, DELTA), 0.0)

    lower = jnp.where(row == 0, halo[0], pltpu.roll(here, 1, 0))
    upper = jnp.where(row == rows - 1, halo[1], pltpu.roll(here, rows - 1, 0))
    prior = step_to(lower, row + me > 0)
    prior = prior + step_to(upper, row + (me + 1 - n_dev) < rows - 1)
    prior = prior + jnp.clip(here - pltpu.roll(here, plane // 2, 1), -DELTA, DELTA)
    prior = prior + step_to(pltpu.roll(here, 1, 1), column > 0)
    prior = prior + step_to(pltpu.roll(here, plane - 1, 1), column < plane // 2 - 1)
    prior = PRIOR_WEIGHT * prior
    for piece in range(pieces):
        at_column = ((piece % 2) * (pieces // 2) + piece // 2) * 128
        prior_ref[pl.ds(piece, rows, stride=pieces), :] = prior[:, at_column : at_column + 128]

    @pl.when(gives_half)
    def _():
        gbox_copy.wait_recv()
        gfwd_copy.start()

    pg_copies[4].wait_recv()
    total = gwin[8 + core] + from_partner[4]
    for j in range(4):

        comes = exists(HOPS[j])
        if j == 3:
            comes = jnp.logical_and(comes, jnp.logical_not(takes_half))

            @pl.when(takes_half)
            def _():
                og_half.wait_recv()
                gfwd_copy.wait_recv()

        @pl.when(comes)
        def _(j=j):
            og_copies[BACK[j]].wait_recv()

        total = total + arrived[j].astype(jnp.float32)
    for piece in range(pieces):
        at_column = ((piece % 2) * (pieces // 2) + piece // 2) * 128
        out_ref[pl.ds(piece, rows, stride=pieces), :] = total[:, at_column : at_column + 128]

    for j, hop in enumerate(HOPS):

        @pl.when(direct(hop))
        def _(j=j):
            vol_copies[j].wait_send()

        @pl.when(exists(hop))
        def _(j=j):
            pass_copies[j].wait_send()

        @pl.when(whole(j))
        def _(j=j):
            og_copies[j].wait_send()

    @pl.when(tail)
    def _():
        og_half.wait_send()
        gbox_copy.wait_send()

    @pl.when(gives_half)
    def _():
        gfwd_copy.wait_send()

    @pl.when(boxed)
    def _():
        box_copy.wait_send()

    @pl.when(relay)
    def _():
        fwd_copy.wait_send()

    @pl.when(tail)
    def _():
        step_copy.wait_send()

    pass_copies[4].wait_send()
    for j in range(5):
        pg_copies[j].wait_send()

    @pl.when(has_below)
    def _():
        edge_copies[0].wait_send()

    @pl.when(has_above)
    def _():
        edge_copies[1].wait_send()


def solution(mesh):
    n_grp, n_view = mesh.shape["grp"], mesh.shape["view"]

    def shards(volume, footprint, measured, angle_index, cover, offset, count):
        blocks, slab, strip, width = volume.shape
        views, det, channels = measured.shape
        tables = footprint.shape[0]
        rows, plane = blocks * slab, strip * width
        total_rows = tables * 5 * CORES * rows
        bf, f32 = jnp.bfloat16, jnp.float32
        dma = pltpu.SemaphoreType.DMA
        hbm = pl.BlockSpec(memory_space=pltpu.HBM)
        data, prior = pl.pallas_call(
            lambda *refs: kernel(n_grp, n_view, *refs),
            out_shape=[jax.ShapeDtypeStruct((rows * plane // 128, 128), f32)] * 2,
            in_specs=[hbm] * 7,
            out_specs=[pl.BlockSpec(memory_space=pltpu.VMEM)] * 2,
            scratch_shapes=[
                pltpu.SMEM(angle_index.shape, jnp.int32),
                pltpu.SMEM(cover.T.shape, jnp.int32),
                pltpu.SMEM(offset.T.shape, jnp.int32),
                pltpu.SMEM(count.shape, jnp.int32),
                pltpu.VMEM((rows * plane // 128, 128), f32),
                pltpu.VMEM((rows, plane), f32),
                pltpu.VMEM((tables, plane, channels), bf),
                pltpu.VMEM((views * det, channels), bf),
                pltpu.VMEM((views * det, channels), f32),
                pltpu.VMEM((10, rows, plane), bf),
                pltpu.VMEM((2, 1, plane), f32),
                pltpu.VMEM((2, 1, plane), f32),
                pltpu.VMEM((total_rows, views * det), bf),
                pltpu.VMEM((views * det, total_rows), bf),
                pltpu.VMEM((total_rows, channels), bf),
                pltpu.VMEM((views * det, channels), f32),
                pltpu.VMEM((views * det, channels), bf),
                pltpu.VMEM((total_rows, channels), bf),
                pltpu.VMEM((10, rows, plane), f32),
                pltpu.VMEM((rows, plane), bf),
                pltpu.VMEM((5, rows, plane), f32),
                pltpu.VMEM((4, rows, plane), bf),
                pltpu.VMEM((4, rows, plane), bf),
                dma((7,)),
                dma((4,)),
                dma((4,)),
                dma((5,)),
                dma((5,)),
                dma((2,)),
                dma((2,)),
                dma((5,)),
                dma((5,)),
                dma((4,)),
                dma((4,)),
                dma((1,)),
                dma((1,)),
                dma((2,)),
                pltpu.SemaphoreType.REGULAR((1,)),
                pltpu.SemaphoreType.REGULAR((2,)),
                pltpu.VMEM((rows // 2, plane), bf),
                dma((1,)),
                dma((1,)),
                dma((1,)),
                dma((1,)),
            ],
            compiler_params=pltpu.CompilerParams(
                collective_id=0, has_side_effects=True, vmem_limit_bytes=48 * 1024 * 1024
            ),
            name="ct_gradient",
        )(
            *(
                pltpu.with_memory_space_constraint(array, pltpu.HBM)
                for array in (
                    angle_index,
                    cover.T,
                    offset.T,
                    count,
                    volume.reshape(rows, strip, width // 128, 128).transpose(0, 2, 1, 3).reshape(-1, 128),
                    footprint.reshape(tables, plane, channels),
                    measured.reshape(views * det, channels),
                )
            )
        )
        gradient = data + prior
        return gradient.reshape(rows, width // 128, strip, 128).transpose(0, 2, 1, 3).reshape(volume.shape)

    axes = ("grp", "view")
    in_specs = (
        P(axes, None, None, None),
        P(axes, None, None, None),
        P(axes, None, None),
        P(axes),
        P(axes, None),
        P(axes, None),
        P(axes),
    )
    return jax.shard_map(
        shards, mesh=mesh, in_specs=in_specs, out_specs=P(axes, None, None, None), check_vma=False
    )
```
